512 devices in a mesh: nodes: 64 (over z, x, core), cams: 8 (over y).
Axes of the slice: x: 4, y: 8, z: 8, core: 2. Of those that a mesh axis runs over, the one named last changes fastest.
Arguments:
- iterate: float32 [1024, 12, 128], P(('nodes', 'cams')), may hold values from -6 to 6
- residual: float32 [1024, 12, 128], P(('nodes', 'cams')), may hold values from -6 to 6
- direction: float32 [1024, 12, 128], P(('nodes', 'cams')), may hold values from -5 to 5
- precond: float32 [1024, 12, 128], P(('nodes', 'cams')), may hold values from 0.2 to 6, as said below
- send_list: int32 [64, 64, 3], P('nodes'), may hold values from -1 to 15, as said below
- grads: bfloat16 [12, 1048576], P(None, ('nodes', 'cams')), may hold values from -2.390625 to 2.390625
- node_refs: int32 [4, 1048576], P(None, ('nodes', 'cams')), may hold values from 0 to 24575, as said below
- skin: bfloat16 [4, 1048576], P(None, ('nodes', 'cams')), may hold values from 0.099609375 to 1
- rigid_nbr: int32 [1024, 6, 128], P(('nodes', 'cams')), may hold values from 0 to 127, as said below
Outputs:
- new_iterate: float32 [1024, 12, 128], P(('nodes', 'cams'))
- new_residual: float32 [1024, 12, 128], P(('nodes', 'cams'))
- new_direction: float32 [1024, 12, 128], P(('nodes', 'cams'))
The draws below stay inside these ranges and needn't reach their ends.
Inputs may be any that keep to these rules, and one draw needn't show every extreme that they name: `precond`: Positive. `send_list`: for each owner and receiver the live entries come first and the rest are -1; at most 3 live entries, and every receiver n has all 3 slots live from owner (n - 1) mod 64. `node_refs`: every reference names a live slot of its device's receiver; the 4 references of a pixel lie in the same slot. `rigid_nbr`: never the node itself.
All inputs are finite; a program needn't handle non-finite values.
Results may differ from the reference program's by a relative error of at most 0.00085.
Values sent between devices are 32-bit elements; how exact they have to be, the bound alone decides.
A program may use at most 64 MiB of HBM per device.

```python
import jax
import jax.numpy as jnp
from jax import lax

PARAMS = 12
NPATCH = 128
SKIN = 4
RIG = 6
FRAMES = 8
SLOTS = 3
PIX = 2048
PD = 16
PATCHES = 1024
PIXELS = 1048576
N_NODES = 64
N_CAMS = 8


def live_counts(key):
    base = jax.random.fold_in(key, 7)
    first, second = jax.random.split(base)
    hotness = jax.random.randint(first, (N_NODES,), 0, 4)
    sparse = jax.random.randint(second, (N_NODES, N_NODES), 0, SLOTS // 2 + 1)
    counts = jnp.where(hotness[None, :] == 0, SLOTS, sparse)
    indices = jnp.arange(N_NODES, dtype=jnp.int32)
    forced = indices[None, :] == (indices[:, None] + 1) % N_NODES
    return jnp.where(forced, SLOTS, counts).astype(jnp.int32)


def draw_send_list(key, part):
    counts = live_counts(key)
    chosen = jax.random.randint(jax.random.fold_in(key, 11), (N_NODES, N_NODES, SLOTS), 0, PD)
    positions = jnp.arange(SLOTS, dtype=jnp.int32)
    return jnp.where(positions[None, None, :] < counts[:, :, None], chosen, -1).astype(jnp.int32)


def search_row(running, wanted):
    return jnp.searchsorted(running, wanted, side='right')


def draw_node_refs(key, part):
    counts = live_counts(key)
    positions = jnp.arange(SLOTS, dtype=jnp.int32)
    live = (positions[None, None, :] < counts[:, :, None]).astype(jnp.int32)
    per_receiver = jnp.transpose(live, (1, 0, 2)).reshape(N_NODES, N_NODES * SLOTS)
    running = jnp.cumsum(per_receiver, axis=1)
    totals = running[:, -1]
    devices = N_NODES * N_CAMS
    receiver = jnp.arange(devices, dtype=jnp.int32) // N_CAMS
    streams = jax.random.split(jax.random.fold_in(key, 13), 3)
    wanted = jax.random.randint(streams[0], (devices, PIX), 0, totals[receiver][:, None])
    slot_ids = jax.vmap(search_row)(running[receiver], wanted).astype(jnp.int32)
    base_node = jax.random.randint(streams[1], (1, devices, PIX), 0, NPATCH)
    offsets = jax.random.randint(streams[2], (SKIN, devices, PIX), 0, NPATCH)
    offsets = offsets.at[0].set(0)
    within = (base_node + offsets) % NPATCH
    node_ids = slot_ids[None] * NPATCH + within
    return node_ids.reshape(SKIN, devices * PIX).astype(jnp.int32)


def draw_rigid_nbr(key, part):
    stride = jax.random.randint(jax.random.fold_in(key, 17), (PATCHES, RIG, NPATCH), 1, NPATCH)
    return ((jnp.arange(NPATCH, dtype=jnp.int32)[None, None, :] + stride) % NPATCH).astype(jnp.int32)


def draw_direction(key, part):
    position = jnp.arange(PATCHES, dtype=jnp.float32)[:, None, None] / PATCHES
    ramp = 0.7 * (1.0 + 0.8 * position)
    values = jax.random.normal(jax.random.fold_in(key, 19), (PATCHES, PARAMS, NPATCH), jnp.float32)
    return jnp.clip(values * ramp, -5.0, 5.0)


def draw_precond(key, part):
    position = jnp.arange(PATCHES, dtype=jnp.float32)[:, None, None] / PATCHES
    ramp = 1.0 + 2.0 * position
    spread = jax.random.uniform(jax.random.fold_in(key, 29), (PATCHES, PARAMS, NPATCH), jnp.float32, jnp.log(0.2), jnp.log(2.0))
    values = jnp.exp(spread)
    return jnp.clip(values * ramp, 0.2, 6.0)


def block_levels(stream_key, shape, cuts, low, largest):
    loudness = 1.0
    for dim, shards_of in cuts:
        draws = jax.random.uniform(jax.random.fold_in(jax.random.fold_in(stream_key, 6), dim), (shards_of,), jnp.float32, low / len(cuts), largest / len(cuts))
        loudness = loudness * jnp.repeat(jnp.exp(draws), shape[dim] // shards_of).reshape((-1,) + (1,) * (len(shape) - 1 - dim))
    return loudness


def bell_draw(stream_key, dims, scale, limit, shards=(), held_as=jnp.bfloat16):
    entries = jax.random.normal(stream_key, dims, jnp.float32) * scale
    if len(shards) > 0:
        entries = block_levels(stream_key, dims, shards, -0.22, 0.18) * entries
    return jnp.clip(entries, min=-limit, max=limit).astype(held_as)


def setup_inputs(seed: int = 0) -> dict:
    key_list = jax.random.split(jax.random.key(seed), 10)
    return {
        "iterate": bell_draw(key_list[0], (PATCHES, PARAMS, NPATCH), 1.0, 6.0, ((0, 512),), jnp.float32),
        "residual": bell_draw(key_list[1], (PATCHES, PARAMS, NPATCH), 1.0, 6.0, ((0, 512),), jnp.float32),
        "direction": draw_direction(jax.random.fold_in(key_list[9], 71), 0),
        "precond": draw_precond(jax.random.fold_in(key_list[9], 71), 0),
        "send_list": draw_send_list(jax.random.fold_in(key_list[9], 71), 0),
        "grads": bell_draw(key_list[5], (PARAMS, PIXELS), 0.4, 2.390625, ((1, 512),)),
        "node_refs": draw_node_refs(jax.random.fold_in(key_list[9], 71), 0),
        "skin": jnp.clip(0.099609375 + 0.9003906 * jax.random.uniform(key_list[7], (SKIN, PIXELS), jnp.float32) ** block_levels(key_list[7], (SKIN, PIXELS), ((1, 512),), -0.2, 0.2), 0.099609375, 1.0).astype(jnp.bfloat16),
        "rigid_nbr": draw_rigid_nbr(jax.random.fold_in(key_list[9], 71), 0),
    }


temporal_weight = 0.5
rigid_weight = 0.1


def rigidity_one(patch, neighbours):
    difference = patch[:, None, :] - patch[:, neighbours]
    summed = jnp.sum(difference, axis=1)
    summed = summed.at[:, neighbours].add(-difference)
    return rigid_weight * summed


def temporal(direction):
    frame_step = PATCHES // FRAMES
    padding = jnp.zeros((frame_step,) + direction.shape[1:], jnp.float32)
    earlier = jnp.concatenate([padding, direction[:-frame_step]], 0)
    following = jnp.concatenate([direction[frame_step:], padding], 0)
    return temporal_weight * (2.0 * direction - earlier - following)


def data_term(direction, send_list, grads, node_refs, skin):
    nodewise = jnp.transpose(direction, (0, 2, 1)).reshape(PATCHES * NPATCH, PARAMS)

    def advance(totals, device):
        receiver = device // N_CAMS
        offset = device * PIX
        grad_block = lax.dynamic_slice_in_dim(grads, offset, PIX, 1).astype(jnp.float32).T
        node_ids = lax.dynamic_slice_in_dim(node_refs, offset, PIX, 1)
        weights = lax.dynamic_slice_in_dim(skin, offset, PIX, 1).astype(jnp.float32)
        source = node_ids // (SLOTS * NPATCH)
        slot_ids = (node_ids // NPATCH) % SLOTS
        within = node_ids % NPATCH
        listed = send_list[source, receiver, slot_ids]
        usable = (listed >= 0).astype(jnp.float32)
        row_ids = (source * PD + jnp.maximum(listed, 0)) * NPATCH + within
        values = nodewise[row_ids] * usable[..., None]
        projected = jnp.sum(values * grad_block[None], axis=2)
        response = jnp.sum(weights * projected, axis=0)
        pieces = (weights * usable * response[None])[..., None] * grad_block[None]
        return totals.at[row_ids].add(pieces), None

    totals, _ = lax.scan(advance, jnp.zeros_like(nodewise), jnp.arange(N_NODES * N_CAMS, dtype=jnp.int32))
    return jnp.transpose(totals.reshape(PATCHES, NPATCH, PARAMS), (0, 2, 1))


def reference(iterate, residual, direction, precond, send_list, grads, node_refs, skin, rigid_nbr):
    image_all = data_term(direction, send_list, grads, node_refs, skin)
    image_all = image_all + jax.vmap(rigidity_one)(direction, rigid_nbr) + temporal(direction)
    start_norm = jnp.sum(residual * precond * residual)
    curvature = jnp.sum(direction * image_all)
    step_length = start_norm / curvature
    new_iterate = iterate + step_length * direction
    new_residual = residual - step_length * image_all
    scaled_new = precond * new_residual
    new_norm = jnp.sum(new_residual * scaled_new)
    new_direction = scaled_new + (new_norm / start_norm) * direction
    return new_iterate, new_residual, new_direction
```

```python
import functools

import jax
import jax.numpy as jnp
from jax import lax
from jax.experimental import pallas as pl
from jax.experimental.pallas import tpu as pltpu
from jax.sharding import PartitionSpec as P

MESH = pl.DeviceIdType.MESH
FRAMES = 8
HALVES = 2
temporal_weight = 0.5
rigid_weight = 0.1

OWNED, PIXELS, GRADS, RESID, PREC, SMOOTH, PARTIAL, TOTAL, IMAGE, SUMS = range(10)
VISIBLE, RETURNS, NODE_SUMS = range(3)


def split(value):
    high = value.astype(jnp.bfloat16)
    return high, (value - high.astype(jnp.float32)).astype(jnp.bfloat16)


def dot(left, right, contract):
    return lax.dot_general(left, right, (contract, ((), ())), preferred_element_type=jnp.float32)


def kernel(
    node_count, cam_count, tile,
    iterate, residual, direction, precond, send_list, grads, node_refs, skin, rigid_nbr,
    new_iterate, new_residual, new_direction,
    pixels, grad_send, grad_rows, one_hot, weight,
    owned_recv, resid_recv, prec_recv, smooth_send, smooth_recv, frame_recv,
    owned, owned_resid, owned_prec, owned_smooth,
    chosen, visible_send, visible_recv, table, partial, partial_recv, total, returned, square,
    returns_send, returns_recv, image_send, image_recv, image,
    node_sums, cam_sums, cam_send,
    cam_send_sem, cam_recv_sem, node_send_sem, node_recv_sem, frame_send_sem, frame_recv_sem,
):
    me_node = lax.axis_index("nodes")
    me_cam = lax.axis_index("cams")
    group = me_cam // HALVES
    half = lax.rem(me_cam, HALVES)
    params, local, width = direction.shape
    slots = send_list.shape[0]
    per_group = grad_send.shape[1]
    span = width // HALVES
    rows = per_group * span
    keys = slots * node_count
    pixel_count = node_refs.shape[1]
    held = local * cam_count
    first = group * per_group
    frame_step = node_count // FRAMES

    barrier = pltpu.get_barrier_semaphore()

    def greet_cam(k, carry):
        pl.semaphore_signal(barrier, inc=1, device_id={"cams": lax.rem(me_cam + k, cam_count)}, device_id_type=MESH)
        return carry

    def greet_node(k, carry):
        pl.semaphore_signal(barrier, inc=1, device_id={"nodes": lax.rem(me_node + k, node_count)}, device_id_type=MESH)
        return carry

    lax.fori_loop(1, cam_count, greet_cam, 0)
    lax.fori_loop(1, node_count, greet_node, 0)

    def to_cam(phase, source, target, k):
        slot = lax.rem(cam_count - k, cam_count)
        return pltpu.make_async_remote_copy(
            src_ref=source, dst_ref=target.at[slot],
            send_sem=cam_send_sem.at[phase, k], recv_sem=cam_recv_sem.at[phase, slot],
            device_id={"cams": lax.rem(me_cam + k, cam_count)}, device_id_type=MESH,
        )

    def from_cam(phase, target, k):
        return pltpu.make_async_remote_copy(
            src_ref=target.at[k], dst_ref=target.at[k],
            send_sem=cam_send_sem.at[phase, k], recv_sem=cam_recv_sem.at[phase, k],
            device_id={"cams": lax.rem(me_cam + k, cam_count)}, device_id_type=MESH,
        )

    def to_node(phase, source, target, k, indexed):
        peer = lax.rem(me_node + k, node_count)
        return pltpu.make_async_remote_copy(
            src_ref=source.at[peer] if indexed else source.at[me_node], dst_ref=target.at[me_node],
            send_sem=node_send_sem.at[phase, k], recv_sem=node_recv_sem.at[phase, me_node],
            device_id={"nodes": peer}, device_id_type=MESH,
        )

    def from_node(phase, target, k):
        peer = lax.rem(me_node + k, node_count)
        return pltpu.make_async_remote_copy(
            src_ref=target.at[peer], dst_ref=target.at[peer],
            send_sem=node_send_sem.at[phase, k], recv_sem=node_recv_sem.at[phase, peer],
            device_id={"nodes": peer}, device_id_type=MESH,
        )

    def send_nodes(phase, source, target, indexed=True):
        def one(k, carry):
            to_node(phase, source, target, k, indexed).start()
            return carry
        lax.fori_loop(1, node_count, one, 0)

    def wait_nodes(phase, target):
        def one(k, carry):
            from_node(phase, target, k).wait_recv()
            return carry
        lax.fori_loop(1, node_count, one, 0)

    def near(i):
        return jnp.where(lax.rem(i, 2) == 1, (i + 1) // 2, lax.rem(cam_count - i // 2, cam_count))

    def each_cam(body, reverse=False, start=1):
        def one(i, carry):
            body(near(cam_count - 1 - i if reverse else i))
            return carry
        if reverse:
            lax.fori_loop(0, cam_count - start, one, 0)
        else:
            lax.fori_loop(start, cam_count, one, 0)

    pixels[0, 0:4, :] = node_refs[...].astype(jnp.float32)
    pixels[0, 4:8, :] = skin[...].astype(jnp.float32)
    grad_all = grads[...].astype(jnp.float32)
    for g in range(params // per_group):
        grad_send[g] = grad_all[g * per_group:(g + 1) * per_group]
    grad_rows[0] = grad_send[group]
    visible_send[...] = jnp.zeros_like(visible_send)
    returns_send[...] = jnp.zeros_like(returns_send)
    owned_recv[0] = direction[pl.ds(first, per_group)]
    resid_recv[0] = residual[pl.ds(first, per_group)]
    prec_recv[0] = precond[pl.ds(first, per_group)]

    pl.semaphore_wait(barrier, cam_count - 1 + node_count - 1)

    def peer_group(k):
        return lax.rem(me_cam + k, cam_count) // HALVES

    def peer_params(source, k):
        return source.at[pl.ds(peer_group(k) * per_group, per_group)]

    each_cam(lambda k: to_cam(OWNED, peer_params(direction, k), owned_recv, k).start())

    def to_frame(which):
        by = frame_step if which == 0 else node_count - frame_step
        return pltpu.make_async_remote_copy(
            src_ref=direction, dst_ref=frame_recv.at[which],
            send_sem=frame_send_sem.at[which], recv_sem=frame_recv_sem.at[which],
            device_id={"nodes": lax.rem(me_node + by, node_count)}, device_id_type=MESH,
        )

    to_frame(0).start()
    to_frame(1).start()

    def send_pixels(k):
        to_cam(PIXELS, pixels.at[0], pixels, k).start()
        to_cam(GRADS, grad_send.at[peer_group(k)], grad_rows, k).start()

    each_cam(send_pixels)

    def build(k):
        def one(i, carry):
            at = pl.ds(pl.multiple_of(i * tile, tile), tile)
            block = pixels[k, :, at]
            refs = block[0:4].astype(jnp.int32)
            weights = block[4:8]
            place = refs[0:1] >> 7
            source = (place * 171) >> 9
            key = (place - slots * source) * node_count + source
            hits = lax.broadcasted_iota(jnp.int32, (keys, tile), 0) == key
            one_hot[k, :, at] = jnp.where(hits, 1.0, 0.0).astype(jnp.bfloat16)
            within = (refs & (width - 1)) - half * span
            ids = lax.broadcasted_iota(jnp.int32, (span, tile), 0)
            summed = jnp.zeros((span, tile), jnp.float32)
            for s in range(4):
                summed = summed + jnp.where(ids == within[s:s + 1], weights[s:s + 1], 0.0)
            weight[k, :, at] = summed
            return carry
        lax.fori_loop(0, pixel_count // tile, one, 0)

    build(0)

    wanted = lax.broadcasted_iota(jnp.int32, (held, node_count), 0)
    for j in range(slots):
        listed = send_list[j]
        shifted = lax.rem(listed // local + cam_count - me_cam, cam_count) * local + lax.rem(listed, local)
        shifted = jnp.where(listed >= 0, shifted, -1)
        chosen[:, j * node_count:(j + 1) * node_count] = jnp.where(wanted == shifted, 1.0, 0.0)

    def take_half(value):
        return jnp.where(half == 0, value[:, :span], value[:, span:])

    def gather_owned(received, target):
        for k in range(cam_count):
            for f in range(per_group):
                target[f, k * local:(k + 1) * local, :] = received[k, f]

    def halves(target):
        return jnp.concatenate([take_half(target[f]) for f in range(per_group)], axis=1)

    each_cam(lambda k: from_cam(OWNED, owned_recv, k).wait_recv())
    gather_owned(owned_recv, owned)
    mine = halves(owned)
    one_hot_rows = chosen[...].astype(jnp.bfloat16)
    high, low = split(mine)
    listed_rows = dot(one_hot_rows, high, ((0,), (0,))) + dot(one_hot_rows, low, ((0,), (0,)))
    for j in range(slots):
        visible_send[:, j, 0:rows] = listed_rows[j * node_count:(j + 1) * node_count]
    visible_recv[pl.ds(me_node, 1)] = visible_send[pl.ds(me_node, 1)]
    send_nodes(VISIBLE, visible_send, visible_recv)

    each_cam(lambda k: to_cam(RESID, peer_params(residual, k), resid_recv, k).start())
    each_cam(lambda k: to_cam(PREC, peer_params(precond, k), prec_recv, k).start())
    to_frame(0).wait_recv()
    to_frame(1).wait_recv()
    ids = lax.broadcasted_iota(jnp.int32, (width, width), 0)
    lanes = lax.broadcasted_iota(jnp.int32, (width, width), 1)
    identity = jnp.where(ids == lanes, 1.0, 0.0)
    has_earlier = jnp.where(me_node >= frame_step, 1.0, 0.0)
    has_following = jnp.where(me_node < node_count - frame_step, 1.0, 0.0)
    for q in range(local):
        edges = jnp.concatenate(
            [identity - jnp.where(ids == rigid_nbr[r, q:q + 1, :], 1.0, 0.0) for r in range(rigid_nbr.shape[0])], axis=1
        ).astype(jnp.bfloat16)
        patch = jnp.concatenate([direction[f, q:q + 1, :] for f in range(params)], axis=0)
        high, low = split(patch)
        difference = dot(high, edges, ((1,), (0,))) + dot(low, edges, ((1,), (0,)))
        high, low = split(difference)
        rigid = dot(high, edges, ((1,), (1,))) + dot(low, edges, ((1,), (1,)))
        for f in range(params):
            here = direction[f, q:q + 1, :]
            time = 2.0 * here - has_earlier * frame_recv[0, f, q:q + 1, :] - has_following * frame_recv[1, f, q:q + 1, :]
            smooth_send[f, q:q + 1, :] = rigid_weight * rigid[f:f + 1] + temporal_weight * time
    smooth_recv[0] = smooth_send[pl.ds(first, per_group)]
    each_cam(lambda k: to_cam(SMOOTH, peer_params(smooth_send, k), smooth_recv, k).start())

    def build_peer(k):
        from_cam(PIXELS, pixels, k).wait_recv()
        build(k)

    each_cam(build_peer)

    wait_nodes(VISIBLE, visible_recv)
    for j in range(slots):
        high, low = split(visible_recv[:, j, 0:rows])
        table[j * node_count:(j + 1) * node_count, 0:rows] = high
        table[j * node_count:(j + 1) * node_count, rows:2 * rows] = low

    def project(k):
        @pl.when(k != 0)
        def _():
            from_cam(GRADS, grad_rows, k).wait_recv()

        def one(i, carry):
            at = pl.ds(pl.multiple_of(i * tile, tile), tile)
            picked = dot(table[...], one_hot[k, :, at], ((0,), (0,)))
            g = grad_rows[k, :, at]
            summed = jnp.zeros((span, tile), jnp.float32)
            for f in range(per_group):
                piece = picked[f * span:(f + 1) * span] + picked[rows + f * span:rows + (f + 1) * span]
                summed = summed + piece * g[f:f + 1]
            partial[k, :, at] = jnp.sum(summed * weight[k, :, at], axis=0, keepdims=True)
            return carry
        lax.fori_loop(0, pixel_count // tile, one, 0)

        @pl.when(k != 0)
        def _():
            to_cam(PARTIAL, partial.at[k], partial_recv, k).start()

    each_cam(project, reverse=True, start=0)

    partial_recv[0] = partial[0]
    each_cam(lambda k: from_cam(PARTIAL, partial_recv, k).wait_recv())
    summed = partial_recv[0]
    for k in range(1, cam_count):
        summed = summed + partial_recv[k]
    total[0] = summed
    each_cam(lambda k: to_cam(TOTAL, total.at[0], total, k).start(), reverse=True)

    returned[...] = jnp.zeros_like(returned)

    def give_back(k):
        @pl.when(k != 0)
        def _():
            from_cam(TOTAL, total, k).wait_recv()

        def one(i, carry):
            at = pl.ds(pl.multiple_of(i * tile, tile), tile)
            scaled = grad_rows[k, :, at] * total[k, :, at]
            w = weight[k, :, at]
            products = jnp.concatenate([w * scaled[f:f + 1] for f in range(per_group)], axis=0)
            high, low = split(products)
            both = jnp.concatenate([high, low], axis=0)
            returned[...] += dot(both, one_hot[k, :, at], ((1,), (1,)))
            return carry
        lax.fori_loop(0, pixel_count // tile, one, 0)

    each_cam(give_back, start=0)
    square[...] = jnp.zeros_like(square)
    square[0:rows, 0:keys] = returned[0:rows] + returned[rows:2 * rows]
    by_key = jnp.transpose(square[...])
    for j in range(slots):
        returns_send[:, j, 0:rows] = by_key[j * node_count:(j + 1) * node_count, 0:rows]
    returns_recv[pl.ds(me_node, 1)] = returns_send[pl.ds(me_node, 1)]
    send_nodes(RETURNS, returns_send, returns_recv)

    start_norm = jnp.sum(residual[...] * precond[...] * residual[...], axis=(0, 1))[None]
    each_cam(lambda k: from_cam(RESID, resid_recv, k).wait_recv())
    each_cam(lambda k: from_cam(PREC, prec_recv, k).wait_recv())
    each_cam(lambda k: from_cam(SMOOTH, smooth_recv, k).wait_recv())
    gather_owned(resid_recv, owned_resid)
    gather_owned(prec_recv, owned_prec)
    gather_owned(smooth_recv, owned_smooth)
    mine = halves(owned)
    mine_prec = halves(owned_prec)
    weighted_resid = halves(owned_resid) * mine_prec

    wait_nodes(RETURNS, returns_recv)
    pieces = halves(owned_smooth)
    one_hot_rows = chosen[...].astype(jnp.bfloat16)
    for j in range(slots):
        high, low = split(returns_recv[:, j, 0:rows])
        part = one_hot_rows[:, j * node_count:(j + 1) * node_count]
        pieces = pieces + dot(part, high, ((1,), (0,))) + dot(part, low, ((1,), (0,)))

    lane = lax.broadcasted_iota(jnp.int32, (1, width), 1)

    def spread(value, which):
        return jnp.where(lane == which, jnp.sum(value), 0.0)

    mine_sums = (
        spread(start_norm, 0) + spread(mine * pieces, 1) + spread(weighted_resid * pieces, 2)
        + spread(mine_prec * pieces * pieces, 3)
    )
    node_sums[pl.ds(me_node, 1)] = mine_sums[None]
    send_nodes(NODE_SUMS, node_sums, node_sums, indexed=False)

    for f in range(per_group):
        piece = pieces[:, f * span:(f + 1) * span]
        doubled = jnp.concatenate([piece, piece], axis=1)
        for k in range(cam_count):
            image_send[k, f] = doubled[k * local:(k + 1) * local]
    image_recv[0] = image_send[0]
    each_cam(lambda k: to_cam(IMAGE, image_send.at[k], image_recv, k).start())

    wait_nodes(NODE_SUMS, node_sums)
    cam_send[0] = jnp.sum(node_sums[...], axis=0)
    cam_sums[0] = cam_send[0]
    each_cam(lambda k: to_cam(SUMS, cam_send.at[0], cam_sums, k).start())

    each_cam(lambda k: from_cam(IMAGE, image_recv, k).wait_recv())
    lane2 = lax.broadcasted_iota(jnp.int32, (local, width), 1)
    for g in range(params // per_group):
        for f in range(per_group):
            sides = [
                image_recv[lax.rem(HALVES * g + s + cam_count - me_cam, cam_count), f] for s in range(HALVES)
            ]
            image[g * per_group + f] = jnp.where(lane2 < span, sides[0], sides[1])

    each_cam(lambda k: from_cam(SUMS, cam_sums, k).wait_recv())
    sums = jnp.sum(cam_sums[...], axis=0)

    def value_of(which):
        return jnp.sum(jnp.where(lane == which, sums, 0.0), axis=1, keepdims=True)

    start, curvature, cross, square_norm = (value_of(which) for which in range(4))
    step = start / curvature
    new_norm = start - 2.0 * step * cross + step * step * square_norm
    ratio = new_norm / start
    for f in range(params):
        new_iterate[f] = iterate[f] + step * direction[f]
        left = residual[f] - step * image[f]
        new_residual[f] = left
        new_direction[f] = precond[f] * left + ratio * direction[f]

    def sent(k):
        to_cam(OWNED, peer_params(direction, k), owned_recv, k).wait_send()
        to_cam(PIXELS, pixels.at[0], pixels, k).wait_send()
        to_cam(GRADS, grad_send.at[peer_group(k)], grad_rows, k).wait_send()
        to_cam(RESID, peer_params(residual, k), resid_recv, k).wait_send()
        to_cam(PREC, peer_params(precond, k), prec_recv, k).wait_send()
        to_cam(SMOOTH, peer_params(smooth_send, k), smooth_recv, k).wait_send()
        to_cam(PARTIAL, partial.at[k], partial_recv, k).wait_send()
        to_cam(TOTAL, total.at[0], total, k).wait_send()
        to_cam(IMAGE, image_send.at[k], image_recv, k).wait_send()
        to_cam(SUMS, cam_send.at[0], cam_sums, k).wait_send()

    each_cam(sent)
    to_frame(0).wait_send()
    to_frame(1).wait_send()

    def sent_node(k, carry):
        to_node(VISIBLE, visible_send, visible_recv, k, True).wait_send()
        to_node(RETURNS, returns_send, returns_recv, k, True).wait_send()
        to_node(NODE_SUMS, node_sums, node_sums, k, False).wait_send()
        return carry

    lax.fori_loop(1, node_count, sent_node, 0)


def solution(mesh):
    node_count, cam_count = mesh.shape["nodes"], mesh.shape["cams"]

    def on_device(iterate, residual, direction, precond, send_list, grads, node_refs, skin, rigid_nbr):
        local, params, width = direction.shape
        pixel_count = node_refs.shape[1]
        slots = send_list.shape[2]
        groups = cam_count // HALVES
        per_group = params // groups
        span = width // HALVES
        rows = per_group * span
        held = local * cam_count
        keys = slots * node_count
        tile = min(512, pixel_count)
        up = lambda size, to: (size + to - 1) // to * to
        side = up(max(rows, keys), 128)
        message = up(rows, 128)
        turn = lambda value: jnp.transpose(value, (1, 0, 2))
        f32, bf16 = jnp.float32, jnp.bfloat16
        slice_shape = (cam_count, per_group, local, width)
        dma = pltpu.SemaphoreType.DMA
        vmem = pl.BlockSpec(memory_space=pltpu.VMEM)
        patch_shape = jax.ShapeDtypeStruct((params, local, width), f32)
        outs = pl.pallas_call(
            functools.partial(kernel, node_count, cam_count, tile),
            out_shape=(patch_shape,) * 3,
            in_specs=[vmem] * 9,
            out_specs=[vmem] * 3,
            scratch_shapes=[
                pltpu.VMEM((cam_count, 8, pixel_count), f32),
                pltpu.VMEM((groups, per_group, pixel_count), f32),
                pltpu.VMEM((cam_count, per_group, pixel_count), f32),
                pltpu.VMEM((cam_count, keys, pixel_count), bf16),
                pltpu.VMEM((cam_count, span, pixel_count), f32),
                pltpu.VMEM(slice_shape, f32),
                pltpu.VMEM(slice_shape, f32),
                pltpu.VMEM(slice_shape, f32),
                pltpu.VMEM((params, local, width), f32),
                pltpu.VMEM(slice_shape, f32),
                pltpu.VMEM((2, params, local, width), f32),
                pltpu.VMEM((per_group, held, width), f32),
                pltpu.VMEM((per_group, held, width), f32),
                pltpu.VMEM((per_group, held, width), f32),
                pltpu.VMEM((per_group, held, width), f32),
                pltpu.VMEM((held, keys), f32),
                pltpu.VMEM((node_count, slots, message), f32),
                pltpu.VMEM((node_count, slots, message), f32),
                pltpu.VMEM((keys, 2 * rows), bf16),
                pltpu.VMEM((cam_count, 1, pixel_count), f32),
                pltpu.VMEM((cam_count, 1, pixel_count), f32),
                pltpu.VMEM((cam_count, 1, pixel_count), f32),
                pltpu.VMEM((2 * rows, keys), f32),
                pltpu.VMEM((side, side), f32),
                pltpu.VMEM((node_count, slots, message), f32),
                pltpu.VMEM((node_count, slots, message), f32),
                pltpu.VMEM(slice_shape, f32),
                pltpu.VMEM(slice_shape, f32),
                pltpu.VMEM((params, local, width), f32),
                pltpu.VMEM((node_count, 1, width), f32),
                pltpu.VMEM((cam_count, 1, width), f32),
                pltpu.VMEM((1, 1, width), f32),
                dma((10, cam_count)),
                dma((10, cam_count)),
                dma((3, node_count)),
                dma((3, node_count)),
                dma((2,)),
                dma((2,)),
            ],
            compiler_params=pltpu.CompilerParams(collective_id=0, has_side_effects=True, vmem_limit_bytes=60 << 20),
            name="cg_step",
        )(
            turn(iterate), turn(residual), turn(direction), turn(precond), jnp.transpose(send_list, (2, 0, 1)),
            grads, node_refs, skin, turn(rigid_nbr),
        )
        return tuple(turn(out) for out in outs)

    spec = P(("nodes", "cams"), None, None)
    split_last = P(None, ("nodes", "cams"))
    return jax.shard_map(
        on_device,
        mesh=mesh,
        in_specs=(spec, spec, spec, spec, P("nodes", None, None), split_last, split_last, split_last, spec),
        out_specs=(spec, spec, spec),
        check_vma=False,
    )
```

```python
import functools

import jax
import jax.numpy as jnp
from jax import lax
from jax.experimental import pallas as pl
from jax.experimental.pallas import tpu as pltpu
from jax.sharding import PartitionSpec as P

MESH = pl.DeviceIdType.MESH
FRAMES = 8
TILES = (512, 1024, 2048)
HALVES = 2
temporal_weight = 0.5
rigid_weight = 0.1

PIXELS, GRADS, TOTAL, OWNED, RESID, PREC, SMOOTH, PARTIAL, IMAGE, SUMS = range(10)
VISIBLE, RETURNS, NODE_SUMS = range(3)


def split(value):
    high = value.astype(jnp.bfloat16)
    return high, (value - high.astype(jnp.float32)).astype(jnp.bfloat16)


def dot(left, right, contract):
    return lax.dot_general(left, right, (contract, ((), ())), preferred_element_type=jnp.float32)


def kernel(
    node_count, cam_count, tiles,
    residual_in, direction_in, precond_in, send_list_in, grads_in, node_refs_in, skin_in, rigid_nbr_in,
    image, factors,
    residual, direction, precond, send_list, grads, node_refs, skin, rigid_nbr,
    pixels, grad_send, grad_rows, one_hot, weight,
    owned_recv, resid_recv, prec_recv, smooth_send, smooth_recv, frame_recv,
    owned, owned_resid, owned_prec, owned_smooth,
    chosen, visible_send, visible_recv, table, partial, partial_recv, total, returned, square,
    returns_send, returns_recv, image_send, image_recv,
    node_sums, cam_sums, cam_send,
    cam_send_sem, cam_recv_sem, slot_sem, node_send_sem, node_recv_sem, frame_send_sem, frame_recv_sem, input_sem,
):
    me_node = lax.axis_index("nodes")
    me_cam = lax.axis_index("cams")
    group = me_cam // HALVES
    half = lax.rem(me_cam, HALVES)
    params, local, width = direction.shape
    slots = send_list.shape[0]
    per_group = grad_send.shape[1]
    span = width // HALVES
    rows = per_group * span
    keys = slots * node_count
    pixel_count = node_refs.shape[1]
    held = local * cam_count
    first = group * per_group
    frame_step = node_count // FRAMES

    pairs = (
        (node_refs_in, node_refs), (skin_in, skin), (grads_in, grads), (direction_in, direction),
        (residual_in, residual), (precond_in, precond), (send_list_in, send_list), (rigid_nbr_in, rigid_nbr),
    )
    inputs = [pltpu.make_async_copy(source, target, input_sem.at[i]) for i, (source, target) in enumerate(pairs)]
    for copy in inputs:
        copy.start()

    barrier = pltpu.get_barrier_semaphore()

    def greet_cam(k, carry):
        pl.semaphore_signal(barrier, inc=1, device_id={"cams": lax.rem(me_cam + k, cam_count)}, device_id_type=MESH)
        return carry

    def greet_node(k, carry):
        pl.semaphore_signal(barrier, inc=1, device_id={"nodes": lax.rem(me_node + k, node_count)}, device_id_type=MESH)
        return carry

    lax.fori_loop(1, cam_count, greet_cam, 0)
    lax.fori_loop(1, node_count, greet_node, 0)

    def to_cam(phase, source, target, k):
        slot = lax.rem(cam_count - k, cam_count)
        return pltpu.make_async_remote_copy(
            src_ref=source, dst_ref=target.at[slot],
            send_sem=cam_send_sem.at[phase], recv_sem=cam_recv_sem.at[phase],
            device_id={"cams": lax.rem(me_cam + k, cam_count)}, device_id_type=MESH,
        )

    def from_cams(phase, target):
        return pltpu.make_async_remote_copy(
            src_ref=target.at[pl.ds(1, cam_count - 1)], dst_ref=target.at[pl.ds(1, cam_count - 1)],
            send_sem=cam_send_sem.at[phase], recv_sem=cam_recv_sem.at[phase],
            device_id={"cams": lax.rem(me_cam + 1, cam_count)}, device_id_type=MESH,
        )

    def to_cam_slot(phase, source, target, k, slot):
        return pltpu.make_async_remote_copy(
            src_ref=source, dst_ref=target.at[slot],
            send_sem=cam_send_sem.at[phase], recv_sem=slot_sem.at[phase, slot],
            device_id={"cams": lax.rem(me_cam + k, cam_count)}, device_id_type=MESH,
        )

    def to_cam_own(phase, source, target, k):
        return to_cam_slot(phase, source, target, k, lax.rem(cam_count - k, cam_count))

    def from_cam(phase, target, k):
        return pltpu.make_async_remote_copy(
            src_ref=target.at[k], dst_ref=target.at[k],
            send_sem=cam_send_sem.at[phase], recv_sem=slot_sem.at[phase, k],
            device_id={"cams": lax.rem(me_cam + k, cam_count)}, device_id_type=MESH,
        )

    def to_node(phase, source, target, k, indexed):
        peer = lax.rem(me_node + k, node_count)
        return pltpu.make_async_remote_copy(
            src_ref=source.at[peer] if indexed else source.at[me_node], dst_ref=target.at[me_node],
            send_sem=node_send_sem.at[phase], recv_sem=node_recv_sem.at[phase],
            device_id={"nodes": peer}, device_id_type=MESH,
        )

    def from_nodes(phase, target):
        return pltpu.make_async_remote_copy(
            src_ref=target.at[pl.ds(0, node_count - 1)], dst_ref=target.at[pl.ds(0, node_count - 1)],
            send_sem=node_send_sem.at[phase], recv_sem=node_recv_sem.at[phase],
            device_id={"nodes": lax.rem(me_node + 1, node_count)}, device_id_type=MESH,
        )

    def send_nodes(phase, source, target, indexed=True):
        def one(k, carry):
            to_node(phase, source, target, k, indexed).start()
            return carry
        lax.fori_loop(1, node_count, one, 0)

    def near(i):
        return jnp.where(lax.rem(i, 2) == 1, (i + 1) // 2, lax.rem(cam_count - i // 2, cam_count))

    def each_cam(body, reverse=False, start=1):
        def one(i, carry):
            body(near(cam_count - 1 - i if reverse else i))
            return carry
        if reverse:
            lax.fori_loop(0, cam_count - start, one, 0)
        else:
            lax.fori_loop(start, cam_count, one, 0)

    for copy in inputs:
        copy.wait()
    pixels[0, 0:4, :] = node_refs[...].astype(jnp.float32)
    pixels[0, 4:8, :] = skin[...].astype(jnp.float32)
    grad_all = grads[...].astype(jnp.float32)
    for g in range(params // per_group):
        grad_send[g] = grad_all[g * per_group:(g + 1) * per_group]
    grad_rows[0] = grad_send[group]
    visible_send[...] = jnp.zeros_like(visible_send)
    returns_send[...] = jnp.zeros_like(returns_send)
    owned_recv[0] = direction[pl.ds(first, per_group)]
    resid_recv[0] = residual[pl.ds(first, per_group)]
    prec_recv[0] = precond[pl.ds(first, per_group)]

    pl.semaphore_wait(barrier, cam_count - 1 + node_count - 1)

    def peer_group(k):
        return lax.rem(me_cam + k, cam_count) // HALVES

    def peer_params(source, k):
        return source.at[pl.ds(peer_group(k) * per_group, per_group)]

    each_cam(lambda k: to_cam(OWNED, peer_params(direction, k), owned_recv, k).start())

    def to_frame(which):
        by = frame_step if which == 0 else node_count - frame_step
        return pltpu.make_async_remote_copy(
            src_ref=direction, dst_ref=frame_recv.at[which],
            send_sem=frame_send_sem.at[which], recv_sem=frame_recv_sem.at[which],
            device_id={"nodes": lax.rem(me_node + by, node_count)}, device_id_type=MESH,
        )

    to_frame(0).start()
    to_frame(1).start()

    down, up = cam_count // 2, (cam_count - 1) // 2

    def relay(distance):
        if 0 <= distance < down:
            to_cam_slot(PIXELS, pixels.at[distance], pixels, cam_count - 1, distance + 1).start()
        if -up < distance <= 0:
            to_cam_slot(PIXELS, pixels.at[distance % cam_count], pixels, 1, cam_count + distance - 1).start()

    def arrive(distance):
        from_cam(PIXELS, pixels, distance % cam_count).wait_recv()
        relay(distance)

    relay(0)
    each_cam(lambda k: to_cam_own(GRADS, grad_send.at[peer_group(k)], grad_rows, k).start())

    tile = tiles[0]

    def build(k):
        def one(i, carry):
            at = pl.ds(pl.multiple_of(i * tile, tile), tile)
            block = pixels[k, :, at]
            refs = block[0:4].astype(jnp.int32)
            weights = block[4:8]
            place = refs[0:1] >> 7
            source = (place * 171) >> 9
            key = (place - slots * source) * node_count + source
            hits = lax.broadcasted_iota(jnp.int32, (keys, tile), 0) == key
            one_hot[k, :, at] = jnp.where(hits, 1.0, 0.0).astype(jnp.bfloat16)
            within = (refs & (width - 1)) - half * span
            ids = lax.broadcasted_iota(jnp.int32, (span, tile), 0)
            summed = jnp.zeros((span, tile), jnp.float32)
            for s in range(4):
                summed = summed + jnp.where(ids == within[s:s + 1], weights[s:s + 1], 0.0)
            weight[k, :, at] = summed
            return carry
        lax.fori_loop(0, pixel_count // tile, one, 0)

    build(0)

    wanted = lax.broadcasted_iota(jnp.int32, (held, node_count), 0)
    for j in range(slots):
        listed = send_list[j]
        shifted = lax.rem(listed // local + cam_count - me_cam, cam_count) * local + lax.rem(listed, local)
        shifted = jnp.where(listed >= 0, shifted, -1)
        chosen[:, j * node_count:(j + 1) * node_count] = jnp.where(wanted == shifted, 1.0, 0.0)

    def take_half(value):
        return jnp.where(half == 0, value[:, :span], value[:, span:])

    def gather_owned(received, target):
        for k in range(cam_count):
            for f in range(per_group):
                target[f, k * local:(k + 1) * local, :] = received[k, f]

    def halves(target):
        return jnp.concatenate([take_half(target[f]) for f in range(per_group)], axis=1)

    from_cams(OWNED, owned_recv).wait_recv()
    gather_owned(owned_recv, owned)
    mine = halves(owned)
    one_hot_rows = chosen[...].astype(jnp.bfloat16)
    high, low = split(mine)
    listed_rows = dot(one_hot_rows, high, ((0,), (0,))) + dot(one_hot_rows, low, ((0,), (0,)))
    for j in range(slots):
        visible_send[:, j, 0:rows] = listed_rows[j * node_count:(j + 1) * node_count]
    visible_recv[pl.ds(me_node, 1)] = visible_send[pl.ds(me_node, 1)]
    send_nodes(VISIBLE, visible_send, visible_recv)
    ring = [d for step in range(1, down + 1) for d in ((step, -step) if step <= up else (step,))]
    for d in ring:
        if abs(d) == 1:
            arrive(d)

    each_cam(lambda k: to_cam(RESID, peer_params(residual, k), resid_recv, k).start())
    each_cam(lambda k: to_cam(PREC, peer_params(precond, k), prec_recv, k).start())
    to_frame(0).wait_recv()
    to_frame(1).wait_recv()
    ids = lax.broadcasted_iota(jnp.int32, (width, width), 0)
    lanes = lax.broadcasted_iota(jnp.int32, (width, width), 1)
    identity = jnp.where(ids == lanes, 1.0, 0.0)
    has_earlier = jnp.where(me_node >= frame_step, 1.0, 0.0)
    has_following = jnp.where(me_node < node_count - frame_step, 1.0, 0.0)
    for q in range(local):
        edges = jnp.concatenate(
            [identity - jnp.where(ids == rigid_nbr[r, q:q + 1, :], 1.0, 0.0) for r in range(rigid_nbr.shape[0])], axis=1
        ).astype(jnp.bfloat16)
        patch = jnp.concatenate([direction[f, q:q + 1, :] for f in range(params)], axis=0)
        high, low = split(patch)
        difference = dot(high, edges, ((1,), (0,))) + dot(low, edges, ((1,), (0,)))
        high, low = split(difference)
        rigid = dot(high, edges, ((1,), (1,))) + dot(low, edges, ((1,), (1,)))
        for f in range(params):
            here = direction[f, q:q + 1, :]
            time = 2.0 * here - has_earlier * frame_recv[0, f, q:q + 1, :] - has_following * frame_recv[1, f, q:q + 1, :]
            smooth_send[f, q:q + 1, :] = rigid_weight * rigid[f:f + 1] + temporal_weight * time
    smooth_recv[0] = smooth_send[pl.ds(first, per_group)]
    each_cam(lambda k: to_cam(SMOOTH, peer_params(smooth_send, k), smooth_recv, k).start())

    for step in range(1, down + 1):
        for d in ring:
            if abs(d) == step + 1:
                arrive(d)
        for d in ring:
            if abs(d) == step:
                build(d % cam_count)

    from_nodes(VISIBLE, visible_recv).wait_recv()
    for j in range(slots):
        square[j * node_count:(j + 1) * node_count, 0:visible_recv.shape[2]] = visible_recv[:, j, :]
    high, low = split(jnp.transpose(square[...])[0:rows, 0:keys])
    table[0:rows] = high
    table[rows:2 * rows] = low

    project_tile = tiles[1]

    def project(k):
        @pl.when(k != 0)
        def _():
            from_cam(GRADS, grad_rows, k).wait_recv()

        def one(i, carry):
            at = pl.ds(pl.multiple_of(i * project_tile, project_tile), project_tile)
            picked = dot(table[...], one_hot[k, :, at], ((1,), (0,)))
            g = grad_rows[k, :, at]
            summed = jnp.zeros((span, project_tile), jnp.float32)
            for f in range(per_group):
                piece = picked[f * span:(f + 1) * span] + picked[rows + f * span:rows + (f + 1) * span]
                summed = summed + piece * g[f:f + 1]
            partial[k, :, at] = jnp.sum(summed * weight[k, :, at], axis=0, keepdims=True)
            return carry
        lax.fori_loop(0, pixel_count // project_tile, one, 0)

        @pl.when(k != 0)
        def _():
            to_cam(PARTIAL, partial.at[k], partial_recv, k).start()

    each_cam(project, reverse=True, start=0)

    partial_recv[0] = partial[0]
    from_cams(PARTIAL, partial_recv).wait_recv()
    summed = partial_recv[0]
    for k in range(1, cam_count):
        summed = summed + partial_recv[k]
    total[0] = summed
    each_cam(lambda k: to_cam_own(TOTAL, total.at[0], total, k).start(), reverse=True)

    returned[...] = jnp.zeros_like(returned)

    back_tile = tiles[2]

    def give_back(k):
        @pl.when(k != 0)
        def _():
            from_cam(TOTAL, total, k).wait_recv()

        def one(i, carry):
            at = pl.ds(pl.multiple_of(i * back_tile, back_tile), back_tile)
            scaled = grad_rows[k, :, at] * total[k, :, at]
            w = weight[k, :, at]
            products = jnp.concatenate([w * scaled[f:f + 1] for f in range(per_group)], axis=0)
            high, low = split(products)
            both = jnp.concatenate([high, low], axis=0)
            returned[...] += dot(both, one_hot[k, :, at], ((1,), (1,)))
            return carry
        lax.fori_loop(0, pixel_count // back_tile, one, 0)

    each_cam(give_back, start=0)
    square[...] = jnp.zeros_like(square)
    square[0:rows, 0:keys] = returned[0:rows] + returned[rows:2 * rows]
    by_key = jnp.transpose(square[...])
    for j in range(slots):
        returns_send[:, j, 0:rows] = by_key[j * node_count:(j + 1) * node_count, 0:rows]
    returns_recv[pl.ds(me_node, 1)] = returns_send[pl.ds(me_node, 1)]
    send_nodes(RETURNS, returns_send, returns_recv)

    start_norm = jnp.sum(residual[...] * precond[...] * residual[...], axis=(0, 1))[None]
    from_cams(RESID, resid_recv).wait_recv()
    from_cams(PREC, prec_recv).wait_recv()
    from_cams(SMOOTH, smooth_recv).wait_recv()
    gather_owned(resid_recv, owned_resid)
    gather_owned(prec_recv, owned_prec)
    gather_owned(smooth_recv, owned_smooth)
    mine = halves(owned)
    mine_prec = halves(owned_prec)
    weighted_resid = halves(owned_resid) * mine_prec

    from_nodes(RETURNS, returns_recv).wait_recv()
    pieces = halves(owned_smooth)
    one_hot_rows = chosen[...].astype(jnp.bfloat16)
    for j in range(slots):
        high, low = split(returns_recv[:, j, 0:rows])
        part = one_hot_rows[:, j * node_count:(j + 1) * node_count]
        pieces = pieces + dot(part, high, ((1,), (0,))) + dot(part, low, ((1,), (0,)))

    lane = lax.broadcasted_iota(jnp.int32, (1, width), 1)

    def spread(value, which):
        return jnp.where(lane == which, jnp.sum(value), 0.0)

    mine_sums = (
        spread(start_norm, 0) + spread(mine * pieces, 1) + spread(weighted_resid * pieces, 2)
        + spread(mine_prec * pieces * pieces, 3)
    )
    node_sums[pl.ds(me_node, 1)] = mine_sums[None]
    send_nodes(NODE_SUMS, node_sums, node_sums, indexed=False)

    for f in range(per_group):
        piece = pieces[:, f * span:(f + 1) * span]
        doubled = jnp.concatenate([piece, piece], axis=1)
        for k in range(cam_count):
            image_send[k, f] = doubled[k * local:(k + 1) * local]
    image_recv[0] = image_send[0]
    each_cam(lambda k: to_cam(IMAGE, image_send.at[k], image_recv, k).start())

    from_nodes(NODE_SUMS, node_sums).wait_recv()
    cam_send[0] = jnp.sum(node_sums[...], axis=0)
    cam_sums[0] = cam_send[0]
    each_cam(lambda k: to_cam(SUMS, cam_send.at[0], cam_sums, k).start())

    from_cams(IMAGE, image_recv).wait_recv()
    lane2 = lax.broadcasted_iota(jnp.int32, (local, width), 1)
    for g in range(params // per_group):
        for f in range(per_group):
            sides = [
                image_recv[lax.rem(HALVES * g + s + cam_count - me_cam, cam_count), f] for s in range(HALVES)
            ]
            image[g * per_group + f] = jnp.where(lane2 < span, sides[0], sides[1])

    from_cams(SUMS, cam_sums).wait_recv()
    sums = jnp.sum(cam_sums[...], axis=0)

    def value_of(which):
        return jnp.sum(jnp.where(lane == which, sums, 0.0), axis=1, keepdims=True)

    start, curvature, cross, square_norm = (value_of(which) for which in range(4))
    step = start / curvature
    new_norm = start - 2.0 * step * cross + step * step * square_norm
    ratio = new_norm / start
    factors[0] = jnp.broadcast_to(step, (local, width))
    factors[1] = jnp.broadcast_to(ratio, (local, width))

    for phase, target in (
        (PIXELS, pixels), (GRADS, grad_rows), (TOTAL, total), (OWNED, owned_recv), (RESID, resid_recv),
        (PREC, prec_recv), (SMOOTH, smooth_recv), (PARTIAL, partial_recv), (IMAGE, image_recv), (SUMS, cam_sums),
    ):
        from_cams(phase, target).wait_send()
    to_frame(0).wait_send()
    to_frame(1).wait_send()
    for phase, target in ((VISIBLE, visible_recv), (RETURNS, returns_recv), (NODE_SUMS, node_sums)):
        from_nodes(phase, target).wait_send()


def solution(mesh):
    node_count, cam_count = mesh.shape["nodes"], mesh.shape["cams"]

    def on_device(iterate, residual, direction, precond, send_list, grads, node_refs, skin, rigid_nbr):
        local, params, width = direction.shape
        pixel_count = node_refs.shape[1]
        slots = send_list.shape[2]
        groups = cam_count // HALVES
        per_group = params // groups
        span = width // HALVES
        rows = per_group * span
        held = local * cam_count
        keys = slots * node_count
        tiles = tuple(min(size, pixel_count) for size in TILES)
        up = lambda size, to: (size + to - 1) // to * to
        side = up(max(rows, keys), 128)
        message = up(rows, 128)
        turn = lambda value: jnp.transpose(value, (1, 0, 2))
        f32, bf16 = jnp.float32, jnp.bfloat16
        slice_shape = (cam_count, per_group, local, width)
        dma = pltpu.SemaphoreType.DMA
        vmem = pl.BlockSpec(memory_space=pltpu.VMEM)
        patch_shape = jax.ShapeDtypeStruct((params, local, width), f32)
        inputs = (
            turn(residual), turn(direction), turn(precond), jnp.transpose(send_list, (2, 0, 1)),
            grads, node_refs, skin, turn(rigid_nbr),
        )
        image, factors = pl.pallas_call(
            functools.partial(kernel, node_count, cam_count, tiles),
            out_shape=(patch_shape, jax.ShapeDtypeStruct((2, local, width), f32)),
            in_specs=[pl.BlockSpec(memory_space=pl.ANY)] * 8,
            out_specs=[vmem] * 2,
            scratch_shapes=[
                *(pltpu.VMEM(value.shape, value.dtype) for value in inputs),
                pltpu.VMEM((cam_count, 8, pixel_count), f32),
                pltpu.VMEM((groups, per_group, pixel_count), f32),
                pltpu.VMEM((cam_count, per_group, pixel_count), f32),
                pltpu.VMEM((cam_count, keys, pixel_count), bf16),
                pltpu.VMEM((cam_count, span, pixel_count), f32),
                pltpu.VMEM(slice_shape, f32),
                pltpu.VMEM(slice_shape, f32),
                pltpu.VMEM(slice_shape, f32),
                pltpu.VMEM((params, local, width), f32),
                pltpu.VMEM(slice_shape, f32),
                pltpu.VMEM((2, params, local, width), f32),
                pltpu.VMEM((per_group, held, width), f32),
                pltpu.VMEM((per_group, held, width), f32),
                pltpu.VMEM((per_group, held, width), f32),
                pltpu.VMEM((per_group, held, width), f32),
                pltpu.VMEM((held, keys), f32),
                pltpu.VMEM((node_count, slots, message), f32),
                pltpu.VMEM((node_count, slots, message), f32),
                pltpu.VMEM((2 * rows, keys), bf16),
                pltpu.VMEM((cam_count, 1, pixel_count), f32),
                pltpu.VMEM((cam_count, 1, pixel_count), f32),
                pltpu.VMEM((cam_count, 1, pixel_count), f32),
                pltpu.VMEM((2 * rows, keys), f32),
                pltpu.VMEM((side, side), f32),
                pltpu.VMEM((node_count, slots, message), f32),
                pltpu.VMEM((node_count, slots, message), f32),
                pltpu.VMEM(slice_shape, f32),
                pltpu.VMEM(slice_shape, f32),
                pltpu.VMEM((node_count, 1, width), f32),
                pltpu.VMEM((cam_count, 1, width), f32),
                pltpu.VMEM((1, 1, width), f32),
                dma((10,)),
                dma((10,)),
                dma((3, cam_count)),
                dma((3,)),
                dma((3,)),
                dma((2,)),
                dma((2,)),
                dma((8,)),
            ],
            compiler_params=pltpu.CompilerParams(collective_id=0, has_side_effects=True, vmem_limit_bytes=60 << 20),
            name="cg_step",
        )(*inputs)
        image = turn(image)
        step, ratio = factors[0][:, None, :], factors[1][:, None, :]
        new_residual = residual - step * image
        return iterate + step * direction, new_residual, precond * new_residual + ratio * direction

    spec = P(("nodes", "cams"), None, None)
    split_last = P(None, ("nodes", "cams"))
    return jax.shard_map(
        on_device,
        mesh=mesh,
        in_specs=(spec, spec, spec, spec, P("nodes", None, None), split_last, split_last, split_last, spec),
        out_specs=(spec, spec, spec),
        check_vma=False,
    )
```

```python
import functools

import jax
import jax.numpy as jnp
from jax import lax
from jax.experimental import pallas as pl
from jax.experimental.pallas import tpu as pltpu
from jax.sharding import PartitionSpec as P

MESH = pl.DeviceIdType.MESH
FRAMES = 8
REACH = 2
TILES = (512, 1024, 2048)
HALVES = 2
temporal_weight = 0.5
rigid_weight = 0.1

PIXELS, GRADS, TOTAL, OWNED, REST, PARTIAL, IMAGE, SUMS = range(8)
VISIBLE, RETURNS, NODE_SUMS = range(3)


def split(value):
    high = value.astype(jnp.bfloat16)
    return high, (value - high.astype(jnp.float32)).astype(jnp.bfloat16)


def dot(left, right, contract):
    return lax.dot_general(left, right, (contract, ((), ())), preferred_element_type=jnp.float32)


def kernel(
    node_count, cam_count, tiles,
    residual_in, direction_in, precond_in, send_list_in, grads_in, node_refs_in, skin_in, rigid_nbr_in,
    image, factors,
    residual, direction, precond, send_list, grads, node_refs, skin, rigid_nbr,
    pixels, grad_send, grad_rows, one_hot, weight,
    owned_recv, rest_send, rest_recv, frame_recv,
    owned, owned_resid, owned_prec, owned_smooth,
    chosen, visible_send, visible_recv, table, partial, partial_recv, total, returned, square,
    returns_send, returns_recv, image_send, image_recv,
    node_sums, cam_sums, cam_send,
    cam_send_sem, cam_recv_sem, slot_sem, node_send_sem, node_recv_sem, frame_send_sem, frame_recv_sem, input_sem,
):
    me_node = lax.axis_index("nodes")
    me_cam = lax.axis_index("cams")
    group = me_cam // HALVES
    half = lax.rem(me_cam, HALVES)
    params, local, width = direction.shape
    slots = send_list.shape[0]
    per_group = grad_send.shape[1]
    span = width // HALVES
    rows = per_group * span
    keys = slots * node_count
    pixel_count = node_refs.shape[1]
    held = local * cam_count
    first = group * per_group
    frame_step = node_count // FRAMES

    pairs = (
        (node_refs_in, node_refs), (skin_in, skin), (grads_in, grads), (direction_in, direction),
        (residual_in, residual), (precond_in, precond), (send_list_in, send_list), (rigid_nbr_in, rigid_nbr),
    )
    inputs = [pltpu.make_async_copy(source, target, input_sem.at[i]) for i, (source, target) in enumerate(pairs)]
    for copy in inputs:
        copy.start()

    barrier = pltpu.get_barrier_semaphore()

    def wrap(value, size):
        return jnp.where(value >= size, value - size, value)

    def each_node(body):
        middle = node_count // 2
        body(middle)

        def both(i, carry):
            body(middle + i)
            body(middle - i)
            return carry

        lax.fori_loop(1, middle, both, 0)

    def cam_peer(k):
        return wrap(me_cam + k, cam_count)

    cam_peers = [me_cam] + [wrap(me_cam + k, cam_count) for k in range(1, cam_count)]
    near_first = [k for d in range(1, cam_count // 2 + 1) for k in sorted({d, cam_count - d})]

    def place(i):
        return jnp.where(lax.rem(i, 2) == 1, (i + 1) // 2, cam_count - i // 2)

    def each_cam(body):
        for k in near_first:
            body(k)

    def greet(**place):
        pl.semaphore_signal(barrier, inc=1, device_id=place, device_id_type=MESH)

    each_node(lambda k: greet(nodes=wrap(me_node + k, node_count)))
    each_cam(lambda k: greet(cams=cam_peers[k]))

    def to_cam(phase, source, target, k):
        slot = cam_count - k
        return pltpu.make_async_remote_copy(
            src_ref=source, dst_ref=target.at[slot],
            send_sem=cam_send_sem.at[phase], recv_sem=cam_recv_sem.at[phase],
            device_id={"cams": cam_peer(k)}, device_id_type=MESH,
        )

    def from_cams(phase, target):
        return pltpu.make_async_remote_copy(
            src_ref=target.at[pl.ds(1, cam_count - 1)], dst_ref=target.at[pl.ds(1, cam_count - 1)],
            send_sem=cam_send_sem.at[phase], recv_sem=cam_recv_sem.at[phase],
            device_id={"cams": cam_peers[1]}, device_id_type=MESH,
        )

    def to_cam_slot(phase, source, target, k, slot):
        return pltpu.make_async_remote_copy(
            src_ref=source, dst_ref=target.at[slot],
            send_sem=cam_send_sem.at[phase], recv_sem=slot_sem.at[phase, slot],
            device_id={"cams": cam_peer(k)}, device_id_type=MESH,
        )

    def to_cam_own(phase, source, target, k):
        return to_cam_slot(phase, source, target, k, cam_count - k)

    def from_cam(phase, target, k):
        return pltpu.make_async_remote_copy(
            src_ref=target.at[k], dst_ref=target.at[k],
            send_sem=cam_send_sem.at[phase], recv_sem=slot_sem.at[phase, k],
            device_id={"cams": cam_peer(k)}, device_id_type=MESH,
        )

    def to_node(phase, source, target, k, indexed):
        peer = wrap(me_node + k, node_count)
        return pltpu.make_async_remote_copy(
            src_ref=source.at[peer] if indexed else source.at[me_node], dst_ref=target.at[me_node],
            send_sem=node_send_sem.at[phase], recv_sem=node_recv_sem.at[phase],
            device_id={"nodes": peer}, device_id_type=MESH,
        )

    def from_nodes(phase, target):
        return pltpu.make_async_remote_copy(
            src_ref=target.at[pl.ds(0, node_count - 1)], dst_ref=target.at[pl.ds(0, node_count - 1)],
            send_sem=node_send_sem.at[phase], recv_sem=node_recv_sem.at[phase],
            device_id={"nodes": lax.rem(me_node + 1, node_count)}, device_id_type=MESH,
        )

    def send_nodes(phase, source, target, indexed=True):
        each_node(lambda k: to_node(phase, source, target, k, indexed).start())

    for copy in inputs:
        copy.wait()
    pixels[0, 0:4, :] = node_refs[...].astype(jnp.float32)
    pixels[0, 4:8, :] = skin[...].astype(jnp.float32)
    grad_all = grads[...].astype(jnp.float32)
    for g in range(params // per_group):
        grad_send[g] = grad_all[g * per_group:(g + 1) * per_group]
    grad_rows[0] = grad_send[group]
    owned_recv[0] = direction[pl.ds(first, per_group)]
    for g in range(params // per_group):
        rest_send[g, 0] = residual[g * per_group:(g + 1) * per_group]
        rest_send[g, 1] = precond[g * per_group:(g + 1) * per_group]

    pl.semaphore_wait(barrier, cam_count - 1 + node_count - 1)

    def peer_group(k):
        return cam_peers[k] // HALVES

    def peer_params(source, k):
        return source.at[pl.ds(peer_group(k) * per_group, per_group)]

    each_cam(lambda k: to_cam(OWNED, peer_params(direction, k), owned_recv, k).start())

    def to_frame(which):
        by = frame_step if which == 0 else node_count - frame_step
        return pltpu.make_async_remote_copy(
            src_ref=direction, dst_ref=frame_recv.at[which],
            send_sem=frame_send_sem.at[which], recv_sem=frame_recv_sem.at[which],
            device_id={"nodes": lax.rem(me_node + by, node_count)}, device_id_type=MESH,
        )

    to_frame(0).start()
    to_frame(1).start()

    down, up = cam_count // 2, (cam_count - 1) // 2
    ring = [d for step in range(1, down + 1) for d in ((step, -step) if step <= up else (step,))]

    def pass_on(have, want):
        to_cam_slot(
            PIXELS, pixels.at[have % cam_count], pixels, (have - want) % cam_count, want % cam_count
        ).start()

    def arrive(distance):
        from_cam(PIXELS, pixels, distance % cam_count).wait_recv()
        for d in ring:
            if abs(d) > REACH and distance == (REACH if d > 0 else -REACH):
                pass_on(distance, d)

    for d in ring:
        if abs(d) <= REACH:
            pass_on(0, d)
    each_cam(lambda k: to_cam_own(GRADS, grad_send.at[peer_group(k)], grad_rows, k).start())

    tile = tiles[0]

    def build(k):
        def one(i, carry):
            at = pl.ds(pl.multiple_of(i * tile, tile), tile)
            block = pixels[k, :, at]
            refs = block[0:4].astype(jnp.int32)
            weights = block[4:8]
            place = refs[0:1] >> 7
            source = (place * 171) >> 9
            key = (place - slots * source) * node_count + source
            hits = lax.broadcasted_iota(jnp.int32, (keys, tile), 0) == key
            one_hot[k, :, at] = jnp.where(hits, 1.0, 0.0).astype(jnp.bfloat16)
            within = (refs & (width - 1)) - half * span
            ids = lax.broadcasted_iota(jnp.int32, (span, tile), 0)
            summed = jnp.zeros((span, tile), jnp.float32)
            for s in range(4):
                summed = summed + jnp.where(ids == within[s:s + 1], weights[s:s + 1], 0.0)
            weight[k, :, at] = summed
            return carry
        lax.fori_loop(0, pixel_count // tile, one, 0)

    build(0)

    wanted = lax.broadcasted_iota(jnp.int32, (held, node_count), 0)
    for j in range(slots):
        listed = send_list[j]
        shifted = lax.rem(listed // local + cam_count - me_cam, cam_count) * local + lax.rem(listed, local)
        shifted = jnp.where(listed >= 0, shifted, -1)
        chosen[:, j * node_count:(j + 1) * node_count] = jnp.where(wanted == shifted, 1.0, 0.0)

    def take_half(value):
        return jnp.where(half == 0, value[:, :span], value[:, span:])

    def gather_owned(received, target, *which):
        for k in range(cam_count):
            for f in range(per_group):
                target[f, k * local:(k + 1) * local, :] = received[(k, *which, f)]

    def halves(target):
        return jnp.concatenate([take_half(target[f]) for f in range(per_group)], axis=1)

    whole, odd = per_group // 2, per_group % 2

    def pack(target, value):
        for j in range(slots):
            part = value[j * node_count:(j + 1) * node_count]
            for p in range(whole):
                target[:, j * whole + p, :] = part[:, p * width:(p + 1) * width]
        if odd:
            at = whole * width
            last = [value[j * node_count:(j + 1) * node_count, at:at + span] for j in range(slots)]
            last = last + [jnp.zeros_like(last[0])] * (slots % 2)
            for i in range(0, slots, 2):
                target[:, slots * whole + i // 2, :] = jnp.concatenate(last[i:i + 2], axis=1)

    def unpack(target, source):
        for j in range(slots):
            at = pl.ds(j * node_count, node_count)
            for p in range(whole):
                target[at, p * width:(p + 1) * width] = source[:, j * whole + p, :]
            if odd:
                pair = source[:, slots * whole + j // 2, :]
                side = span * (j % 2)
                target[at, whole * width:whole * width + span] = pair[:, side:side + span]

    from_cams(OWNED, owned_recv).wait_recv()
    gather_owned(owned_recv, owned)
    mine = halves(owned)
    one_hot_rows = chosen[...].astype(jnp.bfloat16)
    high, low = split(mine)
    listed_rows = dot(one_hot_rows, high, ((0,), (0,))) + dot(one_hot_rows, low, ((0,), (0,)))
    pack(visible_send, listed_rows)
    visible_recv[pl.ds(me_node, 1)] = visible_send[pl.ds(me_node, 1)]
    send_nodes(VISIBLE, visible_send, visible_recv)

    near_count = len([d for d in ring if abs(d) <= REACH])
    for d in ring[:near_count][::-1]:
        arrive(d)

    def build_near(i, carry):
        build(place(i))
        return carry

    lax.fori_loop(1, near_count + 1, build_near, 0)

    from_nodes(VISIBLE, visible_recv).wait_recv()
    unpack(square, visible_recv)
    high, low = split(jnp.transpose(square[...])[0:rows, 0:keys])
    table[0:rows] = high
    table[rows:2 * rows] = low

    project_tile = tiles[1]

    def project(k):
        @pl.when(k != 0)
        def _():
            from_cam(GRADS, grad_rows, k).wait_recv()

        def one(i, carry):
            at = pl.ds(pl.multiple_of(i * project_tile, project_tile), project_tile)
            picked = dot(table[...], one_hot[k, :, at], ((1,), (0,)))
            g = grad_rows[k, :, at]
            summed = jnp.zeros((span, project_tile), jnp.float32)
            for f in range(per_group):
                piece = picked[f * span:(f + 1) * span] + picked[rows + f * span:rows + (f + 1) * span]
                summed = summed + piece * g[f:f + 1]
            partial[k, :, at] = jnp.sum(summed * weight[k, :, at], axis=0, keepdims=True)
            return carry
        lax.fori_loop(0, pixel_count // project_tile, one, 0)

        @pl.when(k != 0)
        def _():
            to_cam(PARTIAL, partial.at[k], partial_recv, k).start()

    middle = [d % cam_count for d in ring[:near_count] if abs(d) > 1]
    last = [d % cam_count for d in ring[near_count:]]
    order = middle + last + [d % cam_count for d in ring if abs(d) == 1] + [0]

    def in_order(i):
        k = jnp.int32(order[0])
        for at, which in enumerate(order):
            k = jnp.where(i == at, which, k)
        return k

    def step_of(i, carry):
        k = in_order(i)

        @pl.when(jnp.logical_and(i >= len(middle), i < len(middle) + len(last)))
        def _():
            from_cam(PIXELS, pixels, k).wait_recv()
            build(k)

        project(k)
        return carry

    lax.fori_loop(0, cam_count, step_of, 0)

    to_frame(0).wait_recv()
    to_frame(1).wait_recv()
    ids = lax.broadcasted_iota(jnp.int32, (width, width), 0)
    lanes = lax.broadcasted_iota(jnp.int32, (width, width), 1)
    identity = jnp.where(ids == lanes, 1.0, 0.0)
    has_earlier = jnp.where(me_node >= frame_step, 1.0, 0.0)
    has_following = jnp.where(me_node < node_count - frame_step, 1.0, 0.0)
    for q in range(local):
        edges = jnp.concatenate(
            [identity - jnp.where(ids == rigid_nbr[r, q:q + 1, :], 1.0, 0.0) for r in range(rigid_nbr.shape[0])], axis=1
        ).astype(jnp.bfloat16)
        patch = jnp.concatenate([direction[f, q:q + 1, :] for f in range(params)], axis=0)
        high, low = split(patch)
        difference = dot(high, edges, ((1,), (0,))) + dot(low, edges, ((1,), (0,)))
        high, low = split(difference)
        rigid = dot(high, edges, ((1,), (1,))) + dot(low, edges, ((1,), (1,)))
        for f in range(params):
            here = direction[f, q:q + 1, :]
            time = 2.0 * here - has_earlier * frame_recv[0, f, q:q + 1, :] - has_following * frame_recv[1, f, q:q + 1, :]
            rest_send[f // per_group, 2, f % per_group, q:q + 1, :] = rigid_weight * rigid[f:f + 1] + temporal_weight * time
    rest_recv[0] = rest_send[group]


    partial_recv[0] = partial[0]
    from_cams(PARTIAL, partial_recv).wait_recv()
    summed = partial_recv[0]
    for k in range(1, cam_count):
        summed = summed + partial_recv[k]
    total[0] = summed
    for k in near_first[::-1]:
        to_cam_own(TOTAL, total.at[0], total, k).start()

    returned[...] = jnp.zeros_like(returned)

    back_tile = tiles[2]

    def give_back(k):
        @pl.when(k != 0)
        def _():
            from_cam(TOTAL, total, k).wait_recv()

        def one(i, carry):
            at = pl.ds(pl.multiple_of(i * back_tile, back_tile), back_tile)
            scaled = grad_rows[k, :, at] * total[k, :, at]
            w = weight[k, :, at]
            products = jnp.concatenate([w * scaled[f:f + 1] for f in range(per_group)], axis=0)
            high, low = split(products)
            both = jnp.concatenate([high, low], axis=0)
            returned[...] += dot(both, one_hot[k, :, at], ((1,), (1,)))
            return carry
        lax.fori_loop(0, pixel_count // back_tile, one, 0)

    each_cam(lambda k: to_cam(REST, rest_send.at[peer_group(k)], rest_recv, k).start())

    def back_step(i, carry):
        give_back(jnp.where(i == 0, 0, place(i)))
        return carry

    lax.fori_loop(0, cam_count, back_step, 0)
    square[...] = jnp.zeros_like(square)
    square[0:rows, 0:keys] = returned[0:rows] + returned[rows:2 * rows]
    by_key = jnp.transpose(square[...])
    pack(returns_send, by_key)
    returns_recv[pl.ds(me_node, 1)] = returns_send[pl.ds(me_node, 1)]
    send_nodes(RETURNS, returns_send, returns_recv)

    start_norm = jnp.sum(residual[...] * precond[...] * residual[...], axis=(0, 1))[None]
    from_cams(REST, rest_recv).wait_recv()
    for which, target in enumerate((owned_resid, owned_prec, owned_smooth)):
        gather_owned(rest_recv, target, which)
    mine = halves(owned)
    mine_prec = halves(owned_prec)
    weighted_resid = halves(owned_resid) * mine_prec

    from_nodes(RETURNS, returns_recv).wait_recv()
    pieces = halves(owned_smooth)
    unpack(square, returns_recv)
    one_hot_rows = chosen[...].astype(jnp.bfloat16)
    high, low = split(square[0:keys, 0:rows])
    pieces = pieces + dot(one_hot_rows, high, ((1,), (0,))) + dot(one_hot_rows, low, ((1,), (0,)))

    lane = lax.broadcasted_iota(jnp.int32, (1, width), 1)

    def spread(value, which):
        return jnp.where(lane == which, jnp.sum(value), 0.0)

    mine_sums = (
        spread(start_norm, 0) + spread(mine * pieces, 1) + spread(weighted_resid * pieces, 2)
        + spread(mine_prec * pieces * pieces, 3)
    )
    node_sums[pl.ds(me_node, 1)] = mine_sums[None]
    send_nodes(NODE_SUMS, node_sums, node_sums, indexed=False)

    for f in range(per_group):
        piece = pieces[:, f * span:(f + 1) * span]
        doubled = jnp.concatenate([piece, piece], axis=1)
        for k in range(cam_count):
            image_send[k, f] = doubled[k * local:(k + 1) * local]
    image_recv[0] = image_send[0]
    each_cam(lambda k: to_cam(IMAGE, image_send.at[k], image_recv, k).start())

    from_nodes(NODE_SUMS, node_sums).wait_recv()
    cam_send[0] = jnp.sum(node_sums[...], axis=0)
    cam_sums[0] = cam_send[0]
    each_cam(lambda k: to_cam(SUMS, cam_send.at[0], cam_sums, k).start())

    from_cams(IMAGE, image_recv).wait_recv()
    lane2 = lax.broadcasted_iota(jnp.int32, (local, width), 1)
    for g in range(params // per_group):
        for f in range(per_group):
            sides = [
                image_recv[lax.rem(HALVES * g + s + cam_count - me_cam, cam_count), f] for s in range(HALVES)
            ]
            image[g * per_group + f] = jnp.where(lane2 < span, sides[0], sides[1])

    from_cams(SUMS, cam_sums).wait_recv()
    sums = jnp.sum(cam_sums[...], axis=0)

    def value_of(which):
        return jnp.sum(jnp.where(lane == which, sums, 0.0), axis=1, keepdims=True)

    start, curvature, cross, square_norm = (value_of(which) for which in range(4))
    step = start / curvature
    new_norm = start - 2.0 * step * cross + step * step * square_norm
    ratio = new_norm / start
    factors[0] = jnp.broadcast_to(step, (local, width))
    factors[1] = jnp.broadcast_to(ratio, (local, width))

    for phase, target in (
        (PIXELS, pixels), (GRADS, grad_rows), (TOTAL, total), (OWNED, owned_recv), (REST, rest_recv),
        (PARTIAL, partial_recv), (IMAGE, image_recv), (SUMS, cam_sums),
    ):
        from_cams(phase, target).wait_send()
    to_frame(0).wait_send()
    to_frame(1).wait_send()
    for phase, target in ((VISIBLE, visible_recv), (RETURNS, returns_recv), (NODE_SUMS, node_sums)):
        from_nodes(phase, target).wait_send()


def solution(mesh):
    node_count, cam_count = mesh.shape["nodes"], mesh.shape["cams"]

    def on_device(iterate, residual, direction, precond, send_list, grads, node_refs, skin, rigid_nbr):
        local, params, width = direction.shape
        pixel_count = node_refs.shape[1]
        slots = send_list.shape[2]
        groups = cam_count // HALVES
        per_group = params // groups
        span = width // HALVES
        rows = per_group * span
        held = local * cam_count
        keys = slots * node_count
        tiles = tuple(min(size, pixel_count) for size in TILES)
        up = lambda size, to: (size + to - 1) // to * to
        side = up(max(rows, keys), 128)
        message = slots * (per_group // 2) + (per_group % 2) * ((slots + 1) // 2)
        turn = lambda value: jnp.transpose(value, (1, 0, 2))
        f32, bf16 = jnp.float32, jnp.bfloat16
        slice_shape = (cam_count, per_group, local, width)
        dma = pltpu.SemaphoreType.DMA
        vmem = pl.BlockSpec(memory_space=pltpu.VMEM)
        patch_shape = jax.ShapeDtypeStruct((params, local, width), f32)
        inputs = (
            turn(residual), turn(direction), turn(precond), jnp.transpose(send_list, (2, 0, 1)),
            grads, node_refs, skin, turn(rigid_nbr),
        )
        image, factors = pl.pallas_call(
            functools.partial(kernel, node_count, cam_count, tiles),
            out_shape=(patch_shape, jax.ShapeDtypeStruct((2, local, width), f32)),
            in_specs=[pl.BlockSpec(memory_space=pl.ANY)] * 8,
            out_specs=[vmem] * 2,
            scratch_shapes=[
                *(pltpu.VMEM(value.shape, value.dtype) for value in inputs),
                pltpu.VMEM((cam_count, 8, pixel_count), f32),
                pltpu.VMEM((groups, per_group, pixel_count), f32),
                pltpu.VMEM((cam_count, per_group, pixel_count), f32),
                pltpu.VMEM((cam_count, keys, pixel_count), bf16),
                pltpu.VMEM((cam_count, span, pixel_count), f32),
                pltpu.VMEM(slice_shape, f32),
                pltpu.VMEM((groups, 3, per_group, local, width), f32),
                pltpu.VMEM((cam_count, 3, per_group, local, width), f32),
                pltpu.VMEM((2, params, local, width), f32),
                pltpu.VMEM((per_group, held, width), f32),
                pltpu.VMEM((per_group, held, width), f32),
                pltpu.VMEM((per_group, held, width), f32),
                pltpu.VMEM((per_group, held, width), f32),
                pltpu.VMEM((held, keys), f32),
                pltpu.VMEM((node_count, message, width), f32),
                pltpu.VMEM((node_count, message, width), f32),
                pltpu.VMEM((2 * rows, keys), bf16),
                pltpu.VMEM((cam_count, 1, pixel_count), f32),
                pltpu.VMEM((cam_count, 1, pixel_count), f32),
                pltpu.VMEM((cam_count, 1, pixel_count), f32),
                pltpu.VMEM((2 * rows, keys), f32),
                pltpu.VMEM((side, side), f32),
                pltpu.VMEM((node_count, message, width), f32),
                pltpu.VMEM((node_count, message, width), f32),
                pltpu.VMEM(slice_shape, f32),
                pltpu.VMEM(slice_shape, f32),
                pltpu.VMEM((node_count, 1, width), f32),
                pltpu.VMEM((cam_count, 1, width), f32),
                pltpu.VMEM((1, 1, width), f32),
                dma((8,)),
                dma((8,)),
                dma((3, cam_count)),
                dma((3,)),
                dma((3,)),
                dma((2,)),
                dma((2,)),
                dma((8,)),
            ],
            compiler_params=pltpu.CompilerParams(collective_id=0, has_side_effects=True, vmem_limit_bytes=60 << 20),
            name="cg_step",
        )(*inputs)
        image = turn(image)
        step, ratio = factors[0][:, None, :], factors[1][:, None, :]
        new_residual = residual - step * image
        return iterate + step * direction, new_residual, precond * new_residual + ratio * direction

    spec = P(("nodes", "cams"), None, None)
    split_last = P(None, ("nodes", "cams"))
    return jax.shard_map(
        on_device,
        mesh=mesh,
        in_specs=(spec, spec, spec, spec, P("nodes", None, None), split_last, split_last, split_last, spec),
        out_specs=(spec, spec, spec),
        check_vma=False,
    )
```

```python
import functools

import jax
import jax.numpy as jnp
from jax import lax
from jax.experimental import pallas as pl
from jax.experimental.pallas import tpu as pltpu
from jax.sharding import PartitionSpec as P

MESH = pl.DeviceIdType.MESH
FRAMES = 8
REACH = 2
TILES = (512, 1024)
PARTS = 2
HALVES = 2
temporal_weight = 0.5
rigid_weight = 0.1

PIXELS, GRADS, TOTAL, TOTAL_B, OWNED, REST, PARTIAL, PARTIAL_B, IMAGE, SUMS = range(10)
VISIBLE, RETURNS, NODE_SUMS = range(3)


def split(value):
    high = value.astype(jnp.bfloat16)
    return high, (value - high.astype(jnp.float32)).astype(jnp.bfloat16)


def dot(left, right, contract):
    return lax.dot_general(left, right, (contract, ((), ())), preferred_element_type=jnp.float32)


def kernel(
    node_count, cam_count, tiles,
    iterate_in, residual_in, direction_in, precond_in, send_list_in, grads_in, node_refs_in, skin_in, rigid_nbr_in,
    result,
    iterate, residual, direction, precond, send_list, grads, node_refs, skin, rigid_nbr,
    pixels, grad_send, grad_rows, one_hot, weight,
    owned_recv, rest_send, rest_recv, frame_recv,
    owned, owned_resid, owned_prec, owned_smooth,
    chosen, visible_send, visible_recv, table, partial, partial_recv, total, returned, square,
    returns_send, returns_recv, image_send, image_recv, image,
    node_sums, cam_sums, cam_send,
    cam_send_sem, cam_recv_sem, slot_sem, node_send_sem, node_recv_sem, frame_send_sem, frame_recv_sem, input_sem,
):
    me_node = lax.axis_index("nodes")
    me_cam = lax.axis_index("cams")
    group = me_cam // HALVES
    half = lax.rem(me_cam, HALVES)
    params, local, width = direction.shape
    slots = send_list.shape[0]
    per_group = grad_send.shape[1]
    span = width // HALVES
    rows = per_group * span
    keys = slots * node_count
    pixel_count = node_refs.shape[1]
    held = local * cam_count
    first = group * per_group
    frame_step = node_count // FRAMES

    pairs = (
        (node_refs_in, node_refs), (skin_in, skin), (grads_in, grads), (direction_in, direction),
        (residual_in, residual), (precond_in, precond), (send_list_in, send_list), (rigid_nbr_in, rigid_nbr),
        (iterate_in, iterate),
    )
    inputs = [pltpu.make_async_copy(source, target, input_sem.at[i]) for i, (source, target) in enumerate(pairs)]
    barrier = pltpu.get_barrier_semaphore()

    def wrap(value, size):
        return jnp.where(value >= size, value - size, value)

    def each_node(body):
        middle = node_count // 2
        body(middle)

        def both(i, carry):
            body(middle + i)
            body(middle - i)
            return carry

        lax.fori_loop(1, middle, both, 0)

    def cam_peer(k):
        return wrap(me_cam + k, cam_count)

    cam_peers = [me_cam] + [wrap(me_cam + k, cam_count) for k in range(1, cam_count)]
    near_first = [k for d in range(1, cam_count // 2 + 1) for k in sorted({d, cam_count - d})]

    def place(i):
        return jnp.where(lax.rem(i, 2) == 1, (i + 1) // 2, cam_count - i // 2)

    def each_cam(body):
        for k in near_first:
            body(k)

    def greet(**place):
        pl.semaphore_signal(barrier, inc=1, device_id=place, device_id_type=MESH)

    each_cam(lambda k: greet(cams=cam_peers[k]))
    for copy in inputs:
        copy.start()
    each_node(lambda k: greet(nodes=wrap(me_node + k, node_count)))

    def to_cam(phase, source, target, k):
        slot = cam_count - k
        return pltpu.make_async_remote_copy(
            src_ref=source, dst_ref=target.at[slot],
            send_sem=cam_send_sem.at[phase], recv_sem=cam_recv_sem.at[phase],
            device_id={"cams": cam_peer(k)}, device_id_type=MESH,
        )

    def from_cams(phase, target):
        return pltpu.make_async_remote_copy(
            src_ref=target.at[pl.ds(1, cam_count - 1)], dst_ref=target.at[pl.ds(1, cam_count - 1)],
            send_sem=cam_send_sem.at[phase], recv_sem=cam_recv_sem.at[phase],
            device_id={"cams": cam_peers[1]}, device_id_type=MESH,
        )

    def to_cam_slot(phase, source, target, k, slot):
        return pltpu.make_async_remote_copy(
            src_ref=source, dst_ref=target.at[slot],
            send_sem=cam_send_sem.at[phase], recv_sem=slot_sem.at[phase, slot],
            device_id={"cams": cam_peer(k)}, device_id_type=MESH,
        )

    def to_cam_own(phase, source, target, k):
        return to_cam_slot(phase, source, target, k, cam_count - k)

    def from_cam(phase, target, k):
        return pltpu.make_async_remote_copy(
            src_ref=target.at[k], dst_ref=target.at[k],
            send_sem=cam_send_sem.at[phase], recv_sem=slot_sem.at[phase, k],
            device_id={"cams": cam_peer(k)}, device_id_type=MESH,
        )

    def to_node(phase, source, target, k, indexed):
        peer = wrap(me_node + k, node_count)
        return pltpu.make_async_remote_copy(
            src_ref=source.at[peer] if indexed else source.at[me_node], dst_ref=target.at[me_node],
            send_sem=node_send_sem.at[phase], recv_sem=node_recv_sem.at[phase],
            device_id={"nodes": peer}, device_id_type=MESH,
        )

    def from_nodes(phase, target):
        return pltpu.make_async_remote_copy(
            src_ref=target.at[pl.ds(0, node_count - 1)], dst_ref=target.at[pl.ds(0, node_count - 1)],
            send_sem=node_send_sem.at[phase], recv_sem=node_recv_sem.at[phase],
            device_id={"nodes": lax.rem(me_node + 1, node_count)}, device_id_type=MESH,
        )

    def send_nodes(phase, source, target, indexed=True):
        each_node(lambda k: to_node(phase, source, target, k, indexed).start())

    for copy in inputs:
        copy.wait()
    pixels[0, 0:4, :] = node_refs[...].astype(jnp.float32)
    pixels[0, 4:8, :] = skin[...].astype(jnp.float32)
    grad_all = grads[...].astype(jnp.float32)
    for g in range(params // per_group):
        grad_send[g] = grad_all[g * per_group:(g + 1) * per_group]
    grad_rows[0] = grad_send[group]
    owned_recv[0] = direction[pl.ds(first, per_group)]
    for g in range(params // per_group):
        rest_send[g, 0] = residual[g * per_group:(g + 1) * per_group]
        rest_send[g, 1] = precond[g * per_group:(g + 1) * per_group]

    pl.semaphore_wait(barrier, cam_count - 1 + node_count - 1)

    def peer_group(k):
        return cam_peers[k] // HALVES

    def peer_params(source, k):
        return source.at[pl.ds(peer_group(k) * per_group, per_group)]

    each_cam(lambda k: to_cam(OWNED, peer_params(direction, k), owned_recv, k).start())

    def to_frame(which):
        by = frame_step if which == 0 else node_count - frame_step
        return pltpu.make_async_remote_copy(
            src_ref=direction, dst_ref=frame_recv.at[which],
            send_sem=frame_send_sem.at[which], recv_sem=frame_recv_sem.at[which],
            device_id={"nodes": lax.rem(me_node + by, node_count)}, device_id_type=MESH,
        )

    to_frame(0).start()
    to_frame(1).start()

    opposite = cam_count // 2
    ring = [d for step in range(1, opposite + 1) for d in ((step, -step) if step < opposite else (step,))]

    def place_of(distance):
        return distance % cam_count

    def side(distance):
        return jnp.where(half == 0, distance % cam_count, -distance % cam_count)

    def arrive(distance):
        from_cam(PIXELS, pixels, place_of(distance)).wait_recv()
        if abs(distance) == REACH:
            on = distance + (1 if distance > 0 else -1)
            if on in ring and abs(on) < opposite:
                to_cam_slot(PIXELS, pixels.at[place_of(distance)], pixels, place_of(distance - on), place_of(on)).start()

    def pass_opposite():
        if REACH < opposite:
            have = side(REACH)
            to_cam_slot(PIXELS, pixels.at[have], pixels, side(REACH - opposite), opposite).start()

    def send_grads(distance):
        k = side(distance)
        to_cam_slot(GRADS, grad_send.at[cam_peer(k) // HALVES], grad_rows, k, side(-distance)).start()

    def pass_grads(distance):
        have = side(-distance)
        from_cam(GRADS, grad_rows, have).wait_recv()
        to_cam_slot(GRADS, grad_rows.at[have], grad_rows, side(1), side(-distance - 1)).start()

    for d in ring[::-1]:
        if abs(d) <= REACH:
            to_cam_slot(PIXELS, pixels.at[0], pixels, place_of(-d), place_of(d)).start()
    for j in range(opposite - 1, 0, -1):
        send_grads(j if j % 2 == 0 else -j)
    send_grads(1)

    tile = tiles[0]

    def build(k):
        def one(i, carry):
            at = pl.ds(pl.multiple_of(i * tile, tile), tile)
            block = pixels[k, :, at]
            refs = block[0:4].astype(jnp.int32)
            weights = block[4:8]
            place = refs[0:1] >> 7
            source = (place * 171) >> 9
            key = (place - slots * source) * node_count + source
            hits = lax.broadcasted_iota(jnp.int32, (keys, tile), 0) == key
            one_hot[k, :, at] = jnp.where(hits, 1.0, 0.0).astype(jnp.bfloat16)
            within = (refs & (width - 1)) - half * span
            ids = lax.broadcasted_iota(jnp.int32, (span, tile), 0)
            summed = jnp.zeros((span, tile), jnp.float32)
            for s in range(4):
                summed = summed + jnp.where(ids == within[s:s + 1], weights[s:s + 1], 0.0)
            weight[k, :, at] = summed
            return carry
        lax.fori_loop(0, pixel_count // tile, one, 0)

    build(0)

    wanted = lax.broadcasted_iota(jnp.int32, (held, node_count), 0)
    for j in range(slots):
        listed = send_list[j]
        shifted = lax.rem(listed // local + cam_count - me_cam, cam_count) * local + lax.rem(listed, local)
        shifted = jnp.where(listed >= 0, shifted, -1)
        chosen[:, j * node_count:(j + 1) * node_count] = jnp.where(wanted == shifted, 1.0, 0.0)

    def take_half(value):
        return jnp.where(half == 0, value[:, :span], value[:, span:])

    def gather_owned(received, target, *which):
        for k in range(cam_count):
            for f in range(per_group):
                target[f, k * local:(k + 1) * local, :] = received[(k, *which, f)]

    def halves(target):
        return jnp.concatenate([take_half(target[f]) for f in range(per_group)], axis=1)

    whole, odd = per_group // 2, per_group % 2

    def pack(target, value):
        for j in range(slots):
            part = value[j * node_count:(j + 1) * node_count]
            for p in range(whole):
                target[:, j * whole + p, :] = part[:, p * width:(p + 1) * width]
        if odd:
            at = whole * width
            last = [value[j * node_count:(j + 1) * node_count, at:at + span] for j in range(slots)]
            last = last + [jnp.zeros_like(last[0])] * (slots % 2)
            for i in range(0, slots, 2):
                target[:, slots * whole + i // 2, :] = jnp.concatenate(last[i:i + 2], axis=1)

    def unpack(target, source):
        for j in range(slots):
            at = pl.ds(j * node_count, node_count)
            for p in range(whole):
                target[at, p * width:(p + 1) * width] = source[:, j * whole + p, :]
            if odd:
                pair = source[:, slots * whole + j // 2, :]
                side = span * (j % 2)
                target[at, whole * width:whole * width + span] = pair[:, side:side + span]

    from_cams(OWNED, owned_recv).wait_recv()
    gather_owned(owned_recv, owned)
    mine = halves(owned)
    one_hot_rows = chosen[...].astype(jnp.bfloat16)
    high, low = split(mine)
    listed_rows = dot(one_hot_rows, high, ((0,), (0,))) + dot(one_hot_rows, low, ((0,), (0,)))
    pack(visible_send, listed_rows)
    visible_recv[pl.ds(me_node, 1)] = visible_send[pl.ds(me_node, 1)]
    send_nodes(VISIBLE, visible_send, visible_recv)

    near_count = len([d for d in ring if abs(d) <= REACH])
    for d in ring[:near_count][::-1]:
        arrive(d)
        if d == REACH:
            pass_opposite()
    def build_near(i, carry):
        build(place(i))
        return carry

    lax.fori_loop(1, near_count + 1, build_near, 0)
    for j in range(1, opposite):
        pass_grads(j)
    to_frame(0).wait_recv()
    to_frame(1).wait_recv()
    ids = lax.broadcasted_iota(jnp.int32, (width, width), 0)
    lanes = lax.broadcasted_iota(jnp.int32, (width, width), 1)
    identity = jnp.where(ids == lanes, 1.0, 0.0)
    has_earlier = jnp.where(me_node >= frame_step, 1.0, 0.0)
    has_following = jnp.where(me_node < node_count - frame_step, 1.0, 0.0)
    for q in range(local):
        edges = jnp.concatenate(
            [identity - jnp.where(ids == rigid_nbr[r, q:q + 1, :], 1.0, 0.0) for r in range(rigid_nbr.shape[0])], axis=1
        ).astype(jnp.bfloat16)
        patch = jnp.concatenate([direction[f, q:q + 1, :] for f in range(params)], axis=0)
        high, low = split(patch)
        difference = dot(high, edges, ((1,), (0,))) + dot(low, edges, ((1,), (0,)))
        high, low = split(difference)
        rigid = dot(high, edges, ((1,), (1,))) + dot(low, edges, ((1,), (1,)))
        for f in range(params):
            here = direction[f, q:q + 1, :]
            time = 2.0 * here - has_earlier * frame_recv[0, f, q:q + 1, :] - has_following * frame_recv[1, f, q:q + 1, :]
            rest_send[f // per_group, 2, f % per_group, q:q + 1, :] = rigid_weight * rigid[f:f + 1] + temporal_weight * time
    rest_recv[0] = rest_send[group]


    def build_far(i, carry):
        k = place(i)
        from_cam(PIXELS, pixels, k).wait_recv()
        build(k)
        return carry

    lax.fori_loop(near_count + 1, cam_count, build_far, 0)

    from_nodes(VISIBLE, visible_recv).wait_recv()
    unpack(square, visible_recv)
    high, low = split(jnp.transpose(square[...])[0:rows, 0:keys])
    table[0:rows] = high
    table[rows:2 * rows] = low

    piece_tile = tiles[1]
    part_count = pixel_count // PARTS

    def project(places, part):
        def awaited(k):
            @pl.when(jnp.logical_and(k != 0, jnp.where(half == 0, k <= opposite, k >= opposite)))
            def _():
                from_cam(GRADS, grad_rows, k).wait_recv()

        def send(k):
            @pl.when(k != 0)
            def _():
                to_cam(PARTIAL + part, partial.at[part, k], partial_recv.at[part], k).start()

        if part == 0:
            for k in places:
                awaited(k)

        def one(i, carry):
            here = pl.ds(pl.multiple_of(i * piece_tile, piece_tile), piece_tile)
            at = pl.ds(pl.multiple_of(part * part_count + i * piece_tile, piece_tile), piece_tile)
            for k in places:
                picked = dot(table[...], one_hot[k, :, at], ((1,), (0,)))
                g = grad_rows[k, :, at]
                summed = jnp.zeros((span, piece_tile), jnp.float32)
                for f in range(per_group):
                    piece = picked[f * span:(f + 1) * span] + picked[rows + f * span:rows + (f + 1) * span]
                    summed = summed + piece * g[f:f + 1]
                partial[part, k, :, here] = jnp.sum(summed * weight[k, :, at], axis=0, keepdims=True)
            return carry
        lax.fori_loop(0, part_count // piece_tile, one, 0)
        for k in places:
            send(k)

    def sum_up(part):
        partial_recv[part, 0] = partial[part, 0]
        from_cams(PARTIAL + part, partial_recv.at[part]).wait_recv()
        summed = partial_recv[part, 0]
        for k in range(1, cam_count):
            summed = summed + partial_recv[part, k]
        total[part, 0] = summed
        for k in near_first[::-1]:
            to_cam_own(TOTAL + part, total.at[part, 0], total.at[part], k).start()

    def give_back(places, part):
        def awaited(k):
            @pl.when(k != 0)
            def _():
                from_cam(TOTAL + part, total.at[part], k).wait_recv()

        for k in places:
            awaited(k)

        def one(i, carry):
            here = pl.ds(pl.multiple_of(i * piece_tile, piece_tile), piece_tile)
            at = pl.ds(pl.multiple_of(part * part_count + i * piece_tile, piece_tile), piece_tile)
            summed = returned[...]
            for k in places:
                scaled = grad_rows[k, :, at] * total[part, k, :, here]
                w = weight[k, :, at]
                products = jnp.concatenate([w * scaled[f:f + 1] for f in range(per_group)], axis=0)
                high, low = split(products)
                both = jnp.concatenate([high, low], axis=0)
                summed = summed + dot(both, one_hot[k, :, at], ((1,), (1,)))
            returned[...] = summed
            return carry
        lax.fori_loop(0, part_count // piece_tile, one, 0)

    def listed(i, places):
        k = jnp.int32(places[0])
        for at, which in enumerate(places):
            k = jnp.where(i == at, which, k)
        return k

    out_order = near_first[::-1] + [0]
    back_order = [0] + near_first

    def project_some(start, stop, part):
        def one(i, carry):
            project([listed(i, out_order[0::2]), listed(i, out_order[1::2])], part)
            return carry
        lax.fori_loop(start, stop, one, 0)

    def give_back_some(start, stop, part):
        def one(i, carry):
            give_back([listed(i, back_order[0::2]), listed(i, back_order[1::2])], part)
            return carry
        lax.fori_loop(start, stop, one, 0)

    pairs_count = cam_count // 2
    late_sum = 1
    project_some(0, pairs_count, 0)
    project_some(0, pairs_count, 1)
    sum_up(0)
    returned[...] = jnp.zeros_like(returned)
    each_cam(lambda k: to_cam(REST, rest_send.at[peer_group(k)], rest_recv, k).start())
    give_back_some(0, late_sum, 0)
    sum_up(1)
    give_back_some(late_sum, pairs_count, 0)
    give_back_some(0, pairs_count, 1)
    square[...] = jnp.zeros_like(square)
    square[0:rows, 0:keys] = returned[0:rows] + returned[rows:2 * rows]
    by_key = jnp.transpose(square[...])
    pack(returns_send, by_key)
    returns_recv[pl.ds(me_node, 1)] = returns_send[pl.ds(me_node, 1)]
    send_nodes(RETURNS, returns_send, returns_recv)

    start_norm = jnp.sum(residual[...] * precond[...] * residual[...], axis=(0, 1))[None]
    from_cams(REST, rest_recv).wait_recv()
    for which, target in enumerate((owned_resid, owned_prec, owned_smooth)):
        gather_owned(rest_recv, target, which)
    mine = halves(owned)
    mine_prec = halves(owned_prec)
    weighted_resid = halves(owned_resid) * mine_prec

    from_nodes(RETURNS, returns_recv).wait_recv()
    pieces = halves(owned_smooth)
    unpack(square, returns_recv)
    one_hot_rows = chosen[...].astype(jnp.bfloat16)
    high, low = split(square[0:keys, 0:rows])
    pieces = pieces + dot(one_hot_rows, high, ((1,), (0,))) + dot(one_hot_rows, low, ((1,), (0,)))

    lane = lax.broadcasted_iota(jnp.int32, (1, width), 1)

    def spread(value, which):
        return jnp.where(lane == which, jnp.sum(value), 0.0)

    mine_sums = (
        spread(start_norm, 0) + spread(mine * pieces, 1) + spread(weighted_resid * pieces, 2)
        + spread(mine_prec * pieces * pieces, 3)
    )
    node_sums[pl.ds(me_node, 1)] = mine_sums[None]
    send_nodes(NODE_SUMS, node_sums, node_sums, indexed=False)

    for f in range(per_group):
        piece = pieces[:, f * span:(f + 1) * span]
        doubled = jnp.concatenate([piece, piece], axis=1)
        for k in range(cam_count):
            image_send[k, f] = doubled[k * local:(k + 1) * local]
    image_recv[0] = image_send[0]
    each_cam(lambda k: to_cam(IMAGE, image_send.at[k], image_recv, k).start())

    from_nodes(NODE_SUMS, node_sums).wait_recv()
    cam_send[0] = jnp.sum(node_sums[...], axis=0)
    cam_sums[0] = cam_send[0]
    each_cam(lambda k: to_cam(SUMS, cam_send.at[0], cam_sums, k).start())

    from_cams(IMAGE, image_recv).wait_recv()
    lane2 = lax.broadcasted_iota(jnp.int32, (local, width), 1)
    for g in range(params // per_group):
        for f in range(per_group):
            sides = [
                image_recv[lax.rem(HALVES * g + s + cam_count - me_cam, cam_count), f] for s in range(HALVES)
            ]
            image[g * per_group + f] = jnp.where(lane2 < span, sides[0], sides[1])

    from_cams(SUMS, cam_sums).wait_recv()
    sums = jnp.sum(cam_sums[...], axis=0)

    def value_of(which):
        return jnp.sum(jnp.where(lane == which, sums, 0.0), axis=1, keepdims=True)

    start, curvature, cross, square_norm = (value_of(which) for which in range(4))
    step = start / curvature
    new_norm = start - 2.0 * step * cross + step * step * square_norm
    ratio = new_norm / start
    for f in range(params):
        left = residual[f] - step * image[f]
        result[f] = iterate[f] + step * direction[f]
        result[params + f] = left
        result[2 * params + f] = precond[f] * left + ratio * direction[f]

    for phase, target in (
        (PIXELS, pixels), (GRADS, grad_rows), (OWNED, owned_recv), (REST, rest_recv),
        (IMAGE, image_recv), (SUMS, cam_sums),
    ):
        from_cams(phase, target).wait_send()
    for part in range(PARTS):
        from_cams(TOTAL + part, total.at[part]).wait_send()
        from_cams(PARTIAL + part, partial_recv.at[part]).wait_send()
    to_frame(0).wait_send()
    to_frame(1).wait_send()
    for phase, target in ((VISIBLE, visible_recv), (RETURNS, returns_recv), (NODE_SUMS, node_sums)):
        from_nodes(phase, target).wait_send()


def solution(mesh):
    node_count, cam_count = mesh.shape["nodes"], mesh.shape["cams"]

    def on_device(iterate, residual, direction, precond, send_list, grads, node_refs, skin, rigid_nbr):
        local, params, width = direction.shape
        pixel_count = node_refs.shape[1]
        slots = send_list.shape[2]
        groups = cam_count // HALVES
        per_group = params // groups
        span = width // HALVES
        rows = per_group * span
        held = local * cam_count
        keys = slots * node_count
        part_count = pixel_count // PARTS
        tiles = (min(TILES[0], pixel_count), min(TILES[1], part_count))
        up = lambda size, to: (size + to - 1) // to * to
        side = up(max(rows, keys), 128)
        message = slots * (per_group // 2) + (per_group % 2) * ((slots + 1) // 2)
        turn = lambda value: jnp.transpose(value, (1, 0, 2))
        f32, bf16 = jnp.float32, jnp.bfloat16
        slice_shape = (cam_count, per_group, local, width)
        dma = pltpu.SemaphoreType.DMA
        vmem = pl.BlockSpec(memory_space=pltpu.VMEM)
        inputs = (
            turn(iterate), turn(residual), turn(direction), turn(precond), jnp.transpose(send_list, (2, 0, 1)),
            grads, node_refs, skin, turn(rigid_nbr),
        )
        result = pl.pallas_call(
            functools.partial(kernel, node_count, cam_count, tiles),
            out_shape=jax.ShapeDtypeStruct((3 * params, local, width), f32),
            in_specs=[pl.BlockSpec(memory_space=pl.ANY)] * 9,
            out_specs=vmem,
            scratch_shapes=[
                *(pltpu.VMEM(value.shape, value.dtype) for value in inputs),
                pltpu.VMEM((cam_count, 8, pixel_count), f32),
                pltpu.VMEM((groups, per_group, pixel_count), f32),
                pltpu.VMEM((cam_count, per_group, pixel_count), f32),
                pltpu.VMEM((cam_count, keys, pixel_count), bf16),
                pltpu.VMEM((cam_count, span, pixel_count), f32),
                pltpu.VMEM(slice_shape, f32),
                pltpu.VMEM((groups, 3, per_group, local, width), f32),
                pltpu.VMEM((cam_count, 3, per_group, local, width), f32),
                pltpu.VMEM((2, params, local, width), f32),
                pltpu.VMEM((per_group, held, width), f32),
                pltpu.VMEM((per_group, held, width), f32),
                pltpu.VMEM((per_group, held, width), f32),
                pltpu.VMEM((per_group, held, width), f32),
                pltpu.VMEM((held, keys), f32),
                pltpu.VMEM((node_count, message, width), f32),
                pltpu.VMEM((node_count, message, width), f32),
                pltpu.VMEM((2 * rows, keys), bf16),
                pltpu.VMEM((PARTS, cam_count, 1, part_count), f32),
                pltpu.VMEM((PARTS, cam_count, 1, part_count), f32),
                pltpu.VMEM((PARTS, cam_count, 1, part_count), f32),
                pltpu.VMEM((2 * rows, keys), f32),
                pltpu.VMEM((side, side), f32),
                pltpu.VMEM((node_count, message, width), f32),
                pltpu.VMEM((node_count, message, width), f32),
                pltpu.VMEM(slice_shape, f32),
                pltpu.VMEM(slice_shape, f32),
                pltpu.VMEM((params, local, width), f32),
                pltpu.VMEM((node_count, 1, width), f32),
                pltpu.VMEM((cam_count, 1, width), f32),
                pltpu.VMEM((1, 1, width), f32),
                dma((10,)),
                dma((10,)),
                dma((4, cam_count)),
                dma((3,)),
                dma((3,)),
                dma((2,)),
                dma((2,)),
                dma((9,)),
            ],
            compiler_params=pltpu.CompilerParams(collective_id=0, has_side_effects=True, vmem_limit_bytes=60 << 20),
            name="cg_step",
        )(*inputs)
        return tuple(turn(result[i * params:(i + 1) * params]) for i in range(3))

    spec = P(("nodes", "cams"), None, None)
    split_last = P(None, ("nodes", "cams"))
    return jax.shard_map(
        on_device,
        mesh=mesh,
        in_specs=(spec, spec, spec, spec, P("nodes", None, None), split_last, split_last, split_last, spec),
        out_specs=(spec, spec, spec),
        check_vma=False,
    )
```

```python
import functools

import jax
import jax.numpy as jnp
from jax import lax
from jax.experimental import pallas as pl
from jax.experimental.pallas import tpu as pltpu
from jax.sharding import PartitionSpec as P

MESH = pl.DeviceIdType.MESH
FRAMES = 8
REACH = 2
TILES = (512, 1024)
PARTS = 2
HALVES = 2
temporal_weight = 0.5
rigid_weight = 0.1

PIXELS, PIXELS_B, GRADS, GRADS_B, TOTAL, TOTAL_B, OWNED, REST, PARTIAL, PARTIAL_B, IMAGE, SUMS = range(12)
VISIBLE, RETURNS, NODE_SUMS = range(3)


def split(value):
    high = value.astype(jnp.bfloat16)
    return high, (value - high.astype(jnp.float32)).astype(jnp.bfloat16)


def dot(left, right, contract):
    return lax.dot_general(left, right, (contract, ((), ())), preferred_element_type=jnp.float32)


def kernel(
    node_count, cam_count, tiles,
    iterate_in, residual_in, direction_in, precond_in, send_list_in, grads_in, node_refs_in, skin_in, rigid_nbr_in,
    result,
    iterate, residual, direction, precond, send_list, grads, node_refs, skin, rigid_nbr,
    pixels, grad_send, grad_rows, one_hot, weight,
    owned_recv, rest_send, rest_recv, frame_recv,
    owned, owned_resid, owned_prec, owned_smooth,
    chosen, visible_send, visible_recv, table, partial, partial_recv, total, returned, square,
    returns_send, returns_recv, image_send, image_recv, image,
    node_sums, cam_sums, cam_send,
    cam_send_sem, cam_recv_sem, slot_sem, node_send_sem, node_recv_sem, frame_send_sem, frame_recv_sem, input_sem,
):
    me_node = lax.axis_index("nodes")
    me_cam = lax.axis_index("cams")
    group = me_cam // HALVES
    half = lax.rem(me_cam, HALVES)
    params, local, width = direction.shape
    slots = send_list.shape[0]
    per_group = grad_send.shape[2]
    span = width // HALVES
    rows = per_group * span
    keys = slots * node_count
    pixel_count = node_refs.shape[1]
    held = local * cam_count
    first = group * per_group
    frame_step = node_count // FRAMES

    pairs = (
        (node_refs_in, node_refs), (skin_in, skin), (grads_in, grads), (direction_in, direction),
        (residual_in, residual), (precond_in, precond), (send_list_in, send_list), (rigid_nbr_in, rigid_nbr),
        (iterate_in, iterate),
    )
    inputs = [pltpu.make_async_copy(source, target, input_sem.at[i]) for i, (source, target) in enumerate(pairs)]
    barrier = pltpu.get_barrier_semaphore()

    def wrap(value, size):
        return jnp.where(value >= size, value - size, value)

    def each_node(body):
        middle = node_count // 2
        body(middle)

        def both(i, carry):
            body(middle + i)
            body(middle - i)
            return carry

        lax.fori_loop(1, middle, both, 0)

    def cam_peer(k):
        return wrap(me_cam + k, cam_count)

    cam_peers = [me_cam] + [wrap(me_cam + k, cam_count) for k in range(1, cam_count)]
    near_first = [k for d in range(1, cam_count // 2 + 1) for k in sorted({d, cam_count - d})]

    def place(i):
        return jnp.where(lax.rem(i, 2) == 1, (i + 1) // 2, cam_count - i // 2)

    def each_cam(body):
        for k in near_first:
            body(k)

    def greet(**place):
        pl.semaphore_signal(barrier, inc=1, device_id=place, device_id_type=MESH)

    each_cam(lambda k: greet(cams=cam_peers[k]))
    for copy in inputs:
        copy.start()
    each_node(lambda k: greet(nodes=wrap(me_node + k, node_count)))

    def to_cam(phase, source, target, k):
        slot = cam_count - k
        return pltpu.make_async_remote_copy(
            src_ref=source, dst_ref=target.at[slot],
            send_sem=cam_send_sem.at[phase], recv_sem=cam_recv_sem.at[phase],
            device_id={"cams": cam_peer(k)}, device_id_type=MESH,
        )

    def from_cams(phase, target):
        return pltpu.make_async_remote_copy(
            src_ref=target.at[pl.ds(1, cam_count - 1)], dst_ref=target.at[pl.ds(1, cam_count - 1)],
            send_sem=cam_send_sem.at[phase], recv_sem=cam_recv_sem.at[phase],
            device_id={"cams": cam_peers[1]}, device_id_type=MESH,
        )

    def to_cam_slot(phase, source, target, k, slot):
        return pltpu.make_async_remote_copy(
            src_ref=source, dst_ref=target.at[slot],
            send_sem=cam_send_sem.at[phase], recv_sem=slot_sem.at[phase, slot],
            device_id={"cams": cam_peer(k)}, device_id_type=MESH,
        )

    def to_cam_own(phase, source, target, k):
        return to_cam_slot(phase, source, target, k, cam_count - k)

    def from_cam(phase, target, k):
        return pltpu.make_async_remote_copy(
            src_ref=target.at[k], dst_ref=target.at[k],
            send_sem=cam_send_sem.at[phase], recv_sem=slot_sem.at[phase, k],
            device_id={"cams": cam_peer(k)}, device_id_type=MESH,
        )

    def to_node(phase, source, target, k, indexed):
        peer = wrap(me_node + k, node_count)
        return pltpu.make_async_remote_copy(
            src_ref=source.at[peer] if indexed else source.at[me_node], dst_ref=target.at[me_node],
            send_sem=node_send_sem.at[phase], recv_sem=node_recv_sem.at[phase],
            device_id={"nodes": peer}, device_id_type=MESH,
        )

    def from_nodes(phase, target):
        return pltpu.make_async_remote_copy(
            src_ref=target.at[pl.ds(0, node_count - 1)], dst_ref=target.at[pl.ds(0, node_count - 1)],
            send_sem=node_send_sem.at[phase], recv_sem=node_recv_sem.at[phase],
            device_id={"nodes": lax.rem(me_node + 1, node_count)}, device_id_type=MESH,
        )

    def send_nodes(phase, source, target, indexed=True):
        each_node(lambda k: to_node(phase, source, target, k, indexed).start())

    for copy in inputs:
        copy.wait()
    part_count = pixel_count // PARTS
    grad_all = grads[...].astype(jnp.float32)
    for part in range(PARTS):
        columns = slice(part * part_count, (part + 1) * part_count)
        pixels[part, 0, 0:4, :] = node_refs[:, columns].astype(jnp.float32)
        pixels[part, 0, 4:8, :] = skin[:, columns].astype(jnp.float32)
        for g in range(params // per_group):
            grad_send[part, g] = grad_all[g * per_group:(g + 1) * per_group, columns]
        grad_rows[part, 0] = grad_send[part, group]
    for g in range(params // per_group):
        rest_send[g, 0] = residual[g * per_group:(g + 1) * per_group]
        rest_send[g, 1] = precond[g * per_group:(g + 1) * per_group]
    owned_recv[0] = direction[pl.ds(first, per_group)]

    pl.semaphore_wait(barrier, cam_count - 1 + node_count - 1)

    def peer_group(k):
        return cam_peers[k] // HALVES

    def peer_params(source, k):
        return source.at[pl.ds(peer_group(k) * per_group, per_group)]

    each_cam(lambda k: to_cam(OWNED, peer_params(direction, k), owned_recv, k).start())

    def to_frame(which):
        by = frame_step if which == 0 else node_count - frame_step
        return pltpu.make_async_remote_copy(
            src_ref=direction, dst_ref=frame_recv.at[which],
            send_sem=frame_send_sem.at[which], recv_sem=frame_recv_sem.at[which],
            device_id={"nodes": lax.rem(me_node + by, node_count)}, device_id_type=MESH,
        )

    to_frame(0).start()
    to_frame(1).start()

    opposite = cam_count // 2
    ring = [d for step in range(1, opposite + 1) for d in ((step, -step) if step < opposite else (step,))]

    def place_of(distance):
        return distance % cam_count

    def side(distance):
        return jnp.where(half == 0, distance % cam_count, -distance % cam_count)

    def arrive(distance, part):
        from_cam(PIXELS + part, pixels.at[part], place_of(distance)).wait_recv()
        on = distance + (1 if distance > 0 else -1)
        if abs(distance) == REACH and abs(on) < opposite:
            to_cam_slot(
                PIXELS + part, pixels.at[part, place_of(distance)], pixels.at[part], place_of(distance - on), place_of(on)
            ).start()

    def pass_opposite(part):
        if REACH < opposite:
            have = side(REACH)
            to_cam_slot(PIXELS + part, pixels.at[part, have], pixels.at[part], side(REACH - opposite), opposite).start()

    def send_grads(distance, part):
        k = side(distance)
        source = grad_send.at[part, cam_peer(k) // HALVES]
        to_cam_slot(GRADS + part, source, grad_rows.at[part], k, side(-distance)).start()

    def pass_grads(distance, part):
        have = side(-distance)
        from_cam(GRADS + part, grad_rows.at[part], have).wait_recv()
        to_cam_slot(GRADS + part, grad_rows.at[part, have], grad_rows.at[part], side(1), side(-distance - 1)).start()

    def send_pixels(part):
        for d in ring[::-1]:
            if abs(d) <= REACH:
                to_cam_slot(PIXELS + part, pixels.at[part, 0], pixels.at[part], place_of(-d), place_of(d)).start()
        for j in range(opposite - 1, 0, -1):
            send_grads(j if j % 2 == 0 else -j, part)
        send_grads(1, part)

    near_ring = [d for d in ring if abs(d) <= REACH]

    def pass_pixels(part):
        for d in near_ring[::-1]:
            arrive(d, part)
            if d == REACH:
                pass_opposite(part)

    send_pixels(0)
    send_pixels(1)

    tile = tiles[0]

    def build(k, part):
        def one(i, carry):
            here = pl.ds(pl.multiple_of(i * tile, tile), tile)
            at = pl.ds(pl.multiple_of(part * part_count + i * tile, tile), tile)
            block = pixels[part, k, :, here]
            refs = block[0:4].astype(jnp.int32)
            weights = block[4:8]
            place = refs[0:1] >> 7
            source = (place * 171) >> 9
            key = (place - slots * source) * node_count + source
            hits = lax.broadcasted_iota(jnp.int32, (keys, tile), 0) == key
            one_hot[k, :, at] = jnp.where(hits, 1.0, 0.0).astype(jnp.bfloat16)
            within = (refs & (width - 1)) - half * span
            ids = lax.broadcasted_iota(jnp.int32, (span, tile), 0)
            summed = jnp.zeros((span, tile), jnp.float32)
            for s in range(4):
                summed = summed + jnp.where(ids == within[s:s + 1], weights[s:s + 1], 0.0)
            weight[k, :, at] = summed
            return carry
        lax.fori_loop(0, part_count // tile, one, 0)

    for part in range(PARTS):
        build(0, part)

    wanted = lax.broadcasted_iota(jnp.int32, (held, node_count), 0)
    for j in range(slots):
        listed = send_list[j]
        shifted = lax.rem(listed // local + cam_count - me_cam, cam_count) * local + lax.rem(listed, local)
        shifted = jnp.where(listed >= 0, shifted, -1)
        chosen[:, j * node_count:(j + 1) * node_count] = jnp.where(wanted == shifted, 1.0, 0.0)

    def take_half(value):
        return jnp.where(half == 0, value[:, :span], value[:, span:])

    def gather_owned(received, target, *which):
        for k in range(cam_count):
            for f in range(per_group):
                target[f, k * local:(k + 1) * local, :] = received[(k, *which, f)]

    def halves(target):
        return jnp.concatenate([take_half(target[f]) for f in range(per_group)], axis=1)

    whole, odd = per_group // 2, per_group % 2

    def pack(target, value):
        for j in range(slots):
            part = value[j * node_count:(j + 1) * node_count]
            for p in range(whole):
                target[:, j * whole + p, :] = part[:, p * width:(p + 1) * width]
        if odd:
            at = whole * width
            last = [value[j * node_count:(j + 1) * node_count, at:at + span] for j in range(slots)]
            last = last + [jnp.zeros_like(last[0])] * (slots % 2)
            for i in range(0, slots, 2):
                target[:, slots * whole + i // 2, :] = jnp.concatenate(last[i:i + 2], axis=1)

    def unpack(target, source):
        for j in range(slots):
            at = pl.ds(j * node_count, node_count)
            for p in range(whole):
                target[at, p * width:(p + 1) * width] = source[:, j * whole + p, :]
            if odd:
                pair = source[:, slots * whole + j // 2, :]
                side = span * (j % 2)
                target[at, whole * width:whole * width + span] = pair[:, side:side + span]

    from_cams(OWNED, owned_recv).wait_recv()
    gather_owned(owned_recv, owned)
    mine = halves(owned)
    one_hot_rows = chosen[...].astype(jnp.bfloat16)
    high, low = split(mine)
    listed_rows = dot(one_hot_rows, high, ((0,), (0,))) + dot(one_hot_rows, low, ((0,), (0,)))
    pack(visible_send, listed_rows)
    visible_recv[pl.ds(me_node, 1)] = visible_send[pl.ds(me_node, 1)]
    send_nodes(VISIBLE, visible_send, visible_recv)

    near_count = len(near_ring)

    def build_near(part):
        def one(i, carry):
            build(place(i), part)
            return carry
        lax.fori_loop(1, near_count + 1, one, 0)

    def build_far(part):
        def one(i, carry):
            k = place(i)
            from_cam(PIXELS + part, pixels.at[part], k).wait_recv()
            build(k, part)
            return carry
        lax.fori_loop(near_count + 1, cam_count, one, 0)

    pass_pixels(0)
    build_near(0)
    for j in range(1, opposite):
        pass_grads(j, 0)
    pass_pixels(1)
    build_near(1)
    for j in range(1, opposite):
        pass_grads(j, 1)
    build_far(0)

    from_nodes(VISIBLE, visible_recv).wait_recv()
    unpack(square, visible_recv)
    high, low = split(jnp.transpose(square[...])[0:rows, 0:keys])
    table[0:rows] = high
    table[rows:2 * rows] = low

    piece_tile = tiles[1]

    def project(places, part):
        def awaited(k):
            @pl.when(jnp.logical_and(k != 0, jnp.where(half == 0, k <= opposite, k >= opposite)))
            def _():
                from_cam(GRADS + part, grad_rows.at[part], k).wait_recv()

        def send(k):
            @pl.when(k != 0)
            def _():
                to_cam(PARTIAL + part, partial.at[part, k], partial_recv.at[part], k).start()

        for k in places:
            awaited(k)

        def one(i, carry):
            here = pl.ds(pl.multiple_of(i * piece_tile, piece_tile), piece_tile)
            at = pl.ds(pl.multiple_of(part * part_count + i * piece_tile, piece_tile), piece_tile)
            for k in places:
                picked = dot(table[...], one_hot[k, :, at], ((1,), (0,)))
                g = grad_rows[part, k, :, here]
                summed = jnp.zeros((span, piece_tile), jnp.float32)
                for f in range(per_group):
                    piece = picked[f * span:(f + 1) * span] + picked[rows + f * span:rows + (f + 1) * span]
                    summed = summed + piece * g[f:f + 1]
                partial[part, k, :, here] = jnp.sum(summed * weight[k, :, at], axis=0, keepdims=True)
            return carry
        lax.fori_loop(0, part_count // piece_tile, one, 0)
        for k in places:
            send(k)

    def sum_up(part):
        partial_recv[part, 0] = partial[part, 0]
        from_cams(PARTIAL + part, partial_recv.at[part]).wait_recv()
        summed = partial_recv[part, 0]
        for k in range(1, cam_count):
            summed = summed + partial_recv[part, k]
        total[part, 0] = summed
        for k in near_first[::-1]:
            to_cam_own(TOTAL + part, total.at[part, 0], total.at[part], k).start()

    def give_back(places, part):
        def awaited(k):
            @pl.when(k != 0)
            def _():
                from_cam(TOTAL + part, total.at[part], k).wait_recv()

        for k in places:
            awaited(k)

        def one(i, carry):
            here = pl.ds(pl.multiple_of(i * piece_tile, piece_tile), piece_tile)
            at = pl.ds(pl.multiple_of(part * part_count + i * piece_tile, piece_tile), piece_tile)
            summed = returned[...]
            for k in places:
                scaled = grad_rows[part, k, :, here] * total[part, k, :, here]
                w = weight[k, :, at]
                products = jnp.concatenate([w * scaled[f:f + 1] for f in range(per_group)], axis=0)
                high, low = split(products)
                both = jnp.concatenate([high, low], axis=0)
                summed = summed + dot(both, one_hot[k, :, at], ((1,), (1,)))
            returned[...] = summed
            return carry
        lax.fori_loop(0, part_count // piece_tile, one, 0)

    def listed(i, places):
        k = jnp.int32(places[0])
        for at, which in enumerate(places):
            k = jnp.where(i == at, which, k)
        return k

    out_order = near_first[::-1] + [0]
    back_order = [0] + near_first

    def project_some(start, stop, part):
        def one(i, carry):
            project([listed(i, out_order[0::2]), listed(i, out_order[1::2])], part)
            return carry
        lax.fori_loop(start, stop, one, 0)

    def give_back_some(start, stop, part):
        def one(i, carry):
            give_back([listed(i, back_order[0::2]), listed(i, back_order[1::2])], part)
            return carry
        lax.fori_loop(start, stop, one, 0)

    pairs_count = cam_count // 2
    late_sum = 1
    project_some(0, pairs_count, 0)
    build_far(1)
    project_some(0, pairs_count, 1)
    sum_up(0)
    returned[...] = jnp.zeros_like(returned)
    to_frame(0).wait_recv()
    to_frame(1).wait_recv()
    ids = lax.broadcasted_iota(jnp.int32, (width, width), 0)
    lanes = lax.broadcasted_iota(jnp.int32, (width, width), 1)
    identity = jnp.where(ids == lanes, 1.0, 0.0)
    has_earlier = jnp.where(me_node >= frame_step, 1.0, 0.0)
    has_following = jnp.where(me_node < node_count - frame_step, 1.0, 0.0)
    for q in range(local):
        edges = jnp.concatenate(
            [identity - jnp.where(ids == rigid_nbr[r, q:q + 1, :], 1.0, 0.0) for r in range(rigid_nbr.shape[0])], axis=1
        ).astype(jnp.bfloat16)
        patch = jnp.concatenate([direction[f, q:q + 1, :] for f in range(params)], axis=0)
        high, low = split(patch)
        difference = dot(high, edges, ((1,), (0,))) + dot(low, edges, ((1,), (0,)))
        high, low = split(difference)
        rigid = dot(high, edges, ((1,), (1,))) + dot(low, edges, ((1,), (1,)))
        for f in range(params):
            here = direction[f, q:q + 1, :]
            time = 2.0 * here - has_earlier * frame_recv[0, f, q:q + 1, :] - has_following * frame_recv[1, f, q:q + 1, :]
            rest_send[f // per_group, 2, f % per_group, q:q + 1, :] = rigid_weight * rigid[f:f + 1] + temporal_weight * time
    rest_recv[0] = rest_send[group]


    each_cam(lambda k: to_cam(REST, rest_send.at[peer_group(k)], rest_recv, k).start())
    give_back_some(0, late_sum, 0)
    sum_up(1)
    give_back_some(late_sum, pairs_count, 0)
    give_back_some(0, pairs_count, 1)
    square[...] = jnp.zeros_like(square)
    square[0:rows, 0:keys] = returned[0:rows] + returned[rows:2 * rows]
    by_key = jnp.transpose(square[...])
    pack(returns_send, by_key)
    returns_recv[pl.ds(me_node, 1)] = returns_send[pl.ds(me_node, 1)]
    send_nodes(RETURNS, returns_send, returns_recv)

    start_norm = jnp.sum(residual[...] * precond[...] * residual[...], axis=(0, 1))[None]
    from_cams(REST, rest_recv).wait_recv()
    for which, target in enumerate((owned_resid, owned_prec, owned_smooth)):
        gather_owned(rest_recv, target, which)
    mine = halves(owned)
    mine_prec = halves(owned_prec)
    weighted_resid = halves(owned_resid) * mine_prec

    from_nodes(RETURNS, returns_recv).wait_recv()
    pieces = halves(owned_smooth)
    unpack(square, returns_recv)
    one_hot_rows = chosen[...].astype(jnp.bfloat16)
    high, low = split(square[0:keys, 0:rows])
    pieces = pieces + dot(one_hot_rows, high, ((1,), (0,))) + dot(one_hot_rows, low, ((1,), (0,)))

    lane = lax.broadcasted_iota(jnp.int32, (1, width), 1)

    def spread(value, which):
        return jnp.where(lane == which, jnp.sum(value), 0.0)

    mine_sums = (
        spread(start_norm, 0) + spread(mine * pieces, 1) + spread(weighted_resid * pieces, 2)
        + spread(mine_prec * pieces * pieces, 3)
    )
    node_sums[pl.ds(me_node, 1)] = mine_sums[None]
    send_nodes(NODE_SUMS, node_sums, node_sums, indexed=False)

    for f in range(per_group):
        piece = pieces[:, f * span:(f + 1) * span]
        doubled = jnp.concatenate([piece, piece], axis=1)
        for k in range(cam_count):
            image_send[k, f] = doubled[k * local:(k + 1) * local]
    image_recv[0] = image_send[0]
    each_cam(lambda k: to_cam(IMAGE, image_send.at[k], image_recv, k).start())

    from_nodes(NODE_SUMS, node_sums).wait_recv()
    cam_send[0] = jnp.sum(node_sums[...], axis=0)
    cam_sums[0] = cam_send[0]
    each_cam(lambda k: to_cam(SUMS, cam_send.at[0], cam_sums, k).start())

    from_cams(IMAGE, image_recv).wait_recv()
    lane2 = lax.broadcasted_iota(jnp.int32, (local, width), 1)
    for g in range(params // per_group):
        for f in range(per_group):
            sides = [
                image_recv[lax.rem(HALVES * g + s + cam_count - me_cam, cam_count), f] for s in range(HALVES)
            ]
            image[g * per_group + f] = jnp.where(lane2 < span, sides[0], sides[1])

    from_cams(SUMS, cam_sums).wait_recv()
    sums = jnp.sum(cam_sums[...], axis=0)

    def value_of(which):
        return jnp.sum(jnp.where(lane == which, sums, 0.0), axis=1, keepdims=True)

    start, curvature, cross, square_norm = (value_of(which) for which in range(4))
    step = start / curvature
    new_norm = start - 2.0 * step * cross + step * step * square_norm
    ratio = new_norm / start
    for f in range(params):
        left = residual[f] - step * image[f]
        result[f] = iterate[f] + step * direction[f]
        result[params + f] = left
        result[2 * params + f] = precond[f] * left + ratio * direction[f]

    for phase, target in (
        (OWNED, owned_recv), (REST, rest_recv),
        (IMAGE, image_recv), (SUMS, cam_sums),
    ):
        from_cams(phase, target).wait_send()
    for part in range(PARTS):
        from_cams(PIXELS + part, pixels.at[part]).wait_send()
        from_cams(GRADS + part, grad_rows.at[part]).wait_send()
        from_cams(TOTAL + part, total.at[part]).wait_send()
        from_cams(PARTIAL + part, partial_recv.at[part]).wait_send()
    to_frame(0).wait_send()
    to_frame(1).wait_send()
    for phase, target in ((VISIBLE, visible_recv), (RETURNS, returns_recv), (NODE_SUMS, node_sums)):
        from_nodes(phase, target).wait_send()


def solution(mesh):
    node_count, cam_count = mesh.shape["nodes"], mesh.shape["cams"]

    def on_device(iterate, residual, direction, precond, send_list, grads, node_refs, skin, rigid_nbr):
        local, params, width = direction.shape
        pixel_count = node_refs.shape[1]
        slots = send_list.shape[2]
        groups = cam_count // HALVES
        per_group = params // groups
        span = width // HALVES
        rows = per_group * span
        held = local * cam_count
        keys = slots * node_count
        part_count = pixel_count // PARTS
        tiles = tuple(min(size, part_count) for size in TILES)
        up = lambda size, to: (size + to - 1) // to * to
        side = up(max(rows, keys), 128)
        message = slots * (per_group // 2) + (per_group % 2) * ((slots + 1) // 2)
        turn = lambda value: jnp.transpose(value, (1, 0, 2))
        f32, bf16 = jnp.float32, jnp.bfloat16
        slice_shape = (cam_count, per_group, local, width)
        dma = pltpu.SemaphoreType.DMA
        vmem = pl.BlockSpec(memory_space=pltpu.VMEM)
        inputs = (
            turn(iterate), turn(residual), turn(direction), turn(precond), jnp.transpose(send_list, (2, 0, 1)),
            grads, node_refs, skin, turn(rigid_nbr),
        )
        result = pl.pallas_call(
            functools.partial(kernel, node_count, cam_count, tiles),
            out_shape=jax.ShapeDtypeStruct((3 * params, local, width), f32),
            in_specs=[pl.BlockSpec(memory_space=pl.ANY)] * 9,
            out_specs=vmem,
            scratch_shapes=[
                *(pltpu.VMEM(value.shape, value.dtype) for value in inputs),
                pltpu.VMEM((PARTS, cam_count, 8, part_count), f32),
                pltpu.VMEM((PARTS, groups, per_group, part_count), f32),
                pltpu.VMEM((PARTS, cam_count, per_group, part_count), f32),
                pltpu.VMEM((cam_count, keys, pixel_count), bf16),
                pltpu.VMEM((cam_count, span, pixel_count), f32),
                pltpu.VMEM(slice_shape, f32),
                pltpu.VMEM((groups, 3, per_group, local, width), f32),
                pltpu.VMEM((cam_count, 3, per_group, local, width), f32),
                pltpu.VMEM((2, params, local, width), f32),
                pltpu.VMEM((per_group, held, width), f32),
                pltpu.VMEM((per_group, held, width), f32),
                pltpu.VMEM((per_group, held, width), f32),
                pltpu.VMEM((per_group, held, width), f32),
                pltpu.VMEM((held, keys), f32),
                pltpu.VMEM((node_count, message, width), f32),
                pltpu.VMEM((node_count, message, width), f32),
                pltpu.VMEM((2 * rows, keys), bf16),
                pltpu.VMEM((PARTS, cam_count, 1, part_count), f32),
                pltpu.VMEM((PARTS, cam_count, 1, part_count), f32),
                pltpu.VMEM((PARTS, cam_count, 1, part_count), f32),
                pltpu.VMEM((2 * rows, keys), f32),
                pltpu.VMEM((side, side), f32),
                pltpu.VMEM((node_count, message, width), f32),
                pltpu.VMEM((node_count, message, width), f32),
                pltpu.VMEM(slice_shape, f32),
                pltpu.VMEM(slice_shape, f32),
                pltpu.VMEM((params, local, width), f32),
                pltpu.VMEM((node_count, 1, width), f32),
                pltpu.VMEM((cam_count, 1, width), f32),
                pltpu.VMEM((1, 1, width), f32),
                dma((12,)),
                dma((12,)),
                dma((6, cam_count)),
                dma((3,)),
                dma((3,)),
                dma((2,)),
                dma((2,)),
                dma((9,)),
            ],
            compiler_params=pltpu.CompilerParams(collective_id=0, has_side_effects=True, vmem_limit_bytes=60 << 20),
            name="cg_step",
        )(*inputs)
        return tuple(turn(result[i * params:(i + 1) * params]) for i in range(3))

    spec = P(("nodes", "cams"), None, None)
    split_last = P(None, ("nodes", "cams"))
    return jax.shard_map(
        on_device,
        mesh=mesh,
        in_specs=(spec, spec, spec, spec, P("nodes", None, None), split_last, split_last, split_last, spec),
        out_specs=(spec, spec, spec),
        check_vma=False,
    )
```

```python
import functools

import jax
import jax.numpy as jnp
from jax import lax
from jax.experimental import pallas as pl
from jax.experimental.pallas import tpu as pltpu
from jax.sharding import PartitionSpec as P

MESH = pl.DeviceIdType.MESH
FRAMES = 8
REACH = 2
TILES = (512, 1024)
PARTS = 2
QUAD = 4
HALVES = 2
temporal_weight = 0.5
rigid_weight = 0.1

PIXELS, PIXELS_B, GRADS, GRADS_B, TOTAL, TOTAL_B, OWNED, REST, PARTIAL, PARTIAL_B, IMAGE, SUMS = range(12)
VISIBLE, RETURNS, NODE_SUMS = range(3)


def split(value):
    high = value.astype(jnp.bfloat16)
    return high, (value - high.astype(jnp.float32)).astype(jnp.bfloat16)


def dot(left, right, contract):
    return lax.dot_general(left, right, (contract, ((), ())), preferred_element_type=jnp.float32)


def kernel(
    node_count, cam_count, tiles,
    iterate_in, residual_in, direction_in, precond_in, send_list_in, grads_in, node_refs_in, skin_in, rigid_nbr_in,
    result,
    iterate, residual, direction, precond, send_list, grads, node_refs, skin, rigid_nbr,
    pixels, grad_send, grad_rows, one_hot, weight,
    owned_recv, rest_send, rest_recv, frame_recv,
    owned, owned_resid, owned_prec, owned_smooth,
    chosen, visible_send, visible_recv, table, partial, partial_recv, total, returned, square,
    returns_send, returns_recv, image_send, image_recv, image,
    node_sums, cam_sums, cam_send,
    cam_send_sem, cam_recv_sem, slot_sem, node_send_sem, node_recv_sem, frame_send_sem, frame_recv_sem, input_sem,
):
    me_node = lax.axis_index("nodes")
    me_cam = lax.axis_index("cams")
    group = me_cam // HALVES
    half = lax.rem(me_cam, HALVES)
    params, local, width = direction.shape
    slots = send_list.shape[0]
    per_group = grad_send.shape[2]
    span = width // HALVES
    rows = per_group * span
    keys = slots * node_count
    pixel_count = node_refs.shape[1]
    held = local * cam_count
    first = group * per_group
    frame_step = node_count // FRAMES

    pairs = (
        (node_refs_in, node_refs), (skin_in, skin), (grads_in, grads), (direction_in, direction),
        (residual_in, residual), (precond_in, precond), (send_list_in, send_list), (rigid_nbr_in, rigid_nbr),
        (iterate_in, iterate),
    )
    inputs = [pltpu.make_async_copy(source, target, input_sem.at[i]) for i, (source, target) in enumerate(pairs)]
    barrier = pltpu.get_barrier_semaphore()

    def wrap(value, size):
        return jnp.where(value >= size, value - size, value)

    def each_node(body):
        middle = node_count // 2
        body(middle)

        def both(i, carry):
            body(middle + i)
            body(middle - i)
            return carry

        lax.fori_loop(1, middle, both, 0)

    def cam_peer(k):
        return wrap(me_cam + k, cam_count)

    cam_peers = [me_cam] + [wrap(me_cam + k, cam_count) for k in range(1, cam_count)]
    near_first = [k for d in range(1, cam_count // 2 + 1) for k in sorted({d, cam_count - d})]

    def place(i):
        return jnp.where(lax.rem(i, 2) == 1, (i + 1) // 2, cam_count - i // 2)

    def each_cam(body):
        for k in near_first:
            body(k)

    def greet(**place):
        pl.semaphore_signal(barrier, inc=1, device_id=place, device_id_type=MESH)

    each_cam(lambda k: greet(cams=cam_peers[k]))
    for copy in inputs:
        copy.start()
    each_node(lambda k: greet(nodes=wrap(me_node + k, node_count)))

    def to_cam(phase, source, target, k):
        slot = cam_count - k
        return pltpu.make_async_remote_copy(
            src_ref=source, dst_ref=target.at[slot],
            send_sem=cam_send_sem.at[phase], recv_sem=cam_recv_sem.at[phase],
            device_id={"cams": cam_peer(k)}, device_id_type=MESH,
        )

    def from_cams(phase, target):
        return pltpu.make_async_remote_copy(
            src_ref=target.at[pl.ds(1, cam_count - 1)], dst_ref=target.at[pl.ds(1, cam_count - 1)],
            send_sem=cam_send_sem.at[phase], recv_sem=cam_recv_sem.at[phase],
            device_id={"cams": cam_peers[1]}, device_id_type=MESH,
        )

    def to_cam_slot(phase, source, target, k, slot):
        return pltpu.make_async_remote_copy(
            src_ref=source, dst_ref=target.at[slot],
            send_sem=cam_send_sem.at[phase], recv_sem=slot_sem.at[phase, slot],
            device_id={"cams": cam_peer(k)}, device_id_type=MESH,
        )

    def to_cam_own(phase, source, target, k):
        return to_cam_slot(phase, source, target, k, cam_count - k)

    def from_cam(phase, target, k):
        return pltpu.make_async_remote_copy(
            src_ref=target.at[k], dst_ref=target.at[k],
            send_sem=cam_send_sem.at[phase], recv_sem=slot_sem.at[phase, k],
            device_id={"cams": cam_peer(k)}, device_id_type=MESH,
        )

    def to_node(phase, source, target, k, indexed):
        peer = wrap(me_node + k, node_count)
        return pltpu.make_async_remote_copy(
            src_ref=source.at[peer] if indexed else source.at[me_node], dst_ref=target.at[me_node],
            send_sem=node_send_sem.at[phase], recv_sem=node_recv_sem.at[phase],
            device_id={"nodes": peer}, device_id_type=MESH,
        )

    def from_nodes(phase, target):
        return pltpu.make_async_remote_copy(
            src_ref=target.at[pl.ds(0, node_count - 1)], dst_ref=target.at[pl.ds(0, node_count - 1)],
            send_sem=node_send_sem.at[phase], recv_sem=node_recv_sem.at[phase],
            device_id={"nodes": lax.rem(me_node + 1, node_count)}, device_id_type=MESH,
        )

    def send_nodes(phase, source, target, indexed=True):
        each_node(lambda k: to_node(phase, source, target, k, indexed).start())

    for copy in inputs:
        copy.wait()
    part_count = pixel_count // PARTS
    grad_all = grads[...].astype(jnp.float32)
    for part in range(PARTS):
        columns = slice(part * part_count, (part + 1) * part_count)
        pixels[part, 0, 0:4, :] = node_refs[:, columns].astype(jnp.float32)
        pixels[part, 0, 4:8, :] = skin[:, columns].astype(jnp.float32)
        for g in range(params // per_group):
            grad_send[part, g] = grad_all[g * per_group:(g + 1) * per_group, columns]
        grad_rows[part, 0] = grad_send[part, group]
    for g in range(params // per_group):
        rest_send[g, 0] = residual[g * per_group:(g + 1) * per_group]
        rest_send[g, 1] = precond[g * per_group:(g + 1) * per_group]
    owned_recv[0] = direction[pl.ds(first, per_group)]

    pl.semaphore_wait(barrier, cam_count - 1 + node_count - 1)

    def peer_group(k):
        return cam_peers[k] // HALVES

    def peer_params(source, k):
        return source.at[pl.ds(peer_group(k) * per_group, per_group)]

    each_cam(lambda k: to_cam(OWNED, peer_params(direction, k), owned_recv, k).start())

    def to_frame(which):
        by = frame_step if which == 0 else node_count - frame_step
        return pltpu.make_async_remote_copy(
            src_ref=direction, dst_ref=frame_recv.at[which],
            send_sem=frame_send_sem.at[which], recv_sem=frame_recv_sem.at[which],
            device_id={"nodes": lax.rem(me_node + by, node_count)}, device_id_type=MESH,
        )

    to_frame(0).start()
    to_frame(1).start()

    opposite = cam_count // 2
    ring = [d for step in range(1, opposite + 1) for d in ((step, -step) if step < opposite else (step,))]

    def place_of(distance):
        return distance % cam_count

    def side(distance):
        return jnp.where(half == 0, distance % cam_count, -distance % cam_count)

    def arrive(distance, part):
        from_cam(PIXELS + part, pixels.at[part], place_of(distance)).wait_recv()
        on = distance + (1 if distance > 0 else -1)
        if abs(distance) == REACH and abs(on) < opposite:
            to_cam_slot(
                PIXELS + part, pixels.at[part, place_of(distance)], pixels.at[part], place_of(distance - on), place_of(on)
            ).start()

    def pass_opposite(part):
        if REACH < opposite:
            have = side(REACH)
            to_cam_slot(PIXELS + part, pixels.at[part, have], pixels.at[part], side(REACH - opposite), opposite).start()

    def send_grads(distance, part):
        k = side(distance)
        source = grad_send.at[part, cam_peer(k) // HALVES]
        to_cam_slot(GRADS + part, source, grad_rows.at[part], k, side(-distance)).start()

    def pass_grads(distance, part):
        have = side(-distance)
        from_cam(GRADS + part, grad_rows.at[part], have).wait_recv()
        to_cam_slot(GRADS + part, grad_rows.at[part, have], grad_rows.at[part], side(1), side(-distance - 1)).start()

    def send_pixels(part):
        for d in ring[::-1]:
            if abs(d) <= REACH:
                to_cam_slot(PIXELS + part, pixels.at[part, 0], pixels.at[part], place_of(-d), place_of(d)).start()
        for j in range(opposite - 1, 0, -1):
            send_grads(j if j % 2 == 0 else -j, part)
        send_grads(1, part)

    near_ring = [d for d in ring if abs(d) <= REACH]

    def pass_pixels(part):
        for d in near_ring[::-1]:
            arrive(d, part)
            if d == REACH:
                pass_opposite(part)

    send_pixels(0)
    send_pixels(1)

    tile = tiles[0]

    def build(k, part):
        def one(i, carry):
            here = pl.ds(pl.multiple_of(i * tile, tile), tile)
            at = pl.ds(pl.multiple_of(part * part_count + i * tile, tile), tile)
            block = pixels[part, k, :, here]
            refs = block[0:4].astype(jnp.int32)
            weights = block[4:8]
            place = refs[0:1] >> 7
            source = (place * 171) >> 9
            key = (place - slots * source) * node_count + source
            hits = lax.broadcasted_iota(jnp.int32, (keys, tile), 0) == key
            one_hot[k, :, at] = jnp.where(hits, 1.0, 0.0).astype(jnp.bfloat16)
            within = (refs & (width - 1)) - half * span
            ids = lax.broadcasted_iota(jnp.int32, (span, tile), 0)
            summed = jnp.zeros((span, tile), jnp.float32)
            for s in range(4):
                summed = summed + jnp.where(ids == within[s:s + 1], weights[s:s + 1], 0.0)
            weight[k, :, at] = summed
            return carry
        lax.fori_loop(0, part_count // tile, one, 0)

    for part in range(PARTS):
        build(0, part)

    wanted = lax.broadcasted_iota(jnp.int32, (held, node_count), 0)
    for j in range(slots):
        listed = send_list[j]
        shifted = lax.rem(listed // local + cam_count - me_cam, cam_count) * local + lax.rem(listed, local)
        shifted = jnp.where(listed >= 0, shifted, -1)
        chosen[:, j * node_count:(j + 1) * node_count] = jnp.where(wanted == shifted, 1.0, 0.0)

    def take_half(value):
        return jnp.where(half == 0, value[:, :span], value[:, span:])

    def gather_owned(received, target, *which):
        for k in range(cam_count):
            for f in range(per_group):
                target[f, k * local:(k + 1) * local, :] = received[(k, *which, f)]

    def halves(target):
        return jnp.concatenate([take_half(target[f]) for f in range(per_group)], axis=1)

    whole, odd = per_group // 2, per_group % 2

    def pack(target, value):
        for j in range(slots):
            part = value[j * node_count:(j + 1) * node_count]
            for p in range(whole):
                target[:, j * whole + p, :] = part[:, p * width:(p + 1) * width]
        if odd:
            at = whole * width
            last = [value[j * node_count:(j + 1) * node_count, at:at + span] for j in range(slots)]
            last = last + [jnp.zeros_like(last[0])] * (slots % 2)
            for i in range(0, slots, 2):
                target[:, slots * whole + i // 2, :] = jnp.concatenate(last[i:i + 2], axis=1)

    def unpack(target, source):
        for j in range(slots):
            at = pl.ds(j * node_count, node_count)
            for p in range(whole):
                target[at, p * width:(p + 1) * width] = source[:, j * whole + p, :]
            if odd:
                pair = source[:, slots * whole + j // 2, :]
                side = span * (j % 2)
                target[at, whole * width:whole * width + span] = pair[:, side:side + span]

    from_cams(OWNED, owned_recv).wait_recv()
    gather_owned(owned_recv, owned)
    mine = halves(owned)
    one_hot_rows = chosen[...].astype(jnp.bfloat16)
    high, low = split(mine)
    listed_rows = dot(one_hot_rows, high, ((0,), (0,))) + dot(one_hot_rows, low, ((0,), (0,)))
    pack(visible_send, listed_rows)
    visible_recv[pl.ds(me_node, 1)] = visible_send[pl.ds(me_node, 1)]
    send_nodes(VISIBLE, visible_send, visible_recv)

    near_count = len(near_ring)

    def build_near(part):
        def one(i, carry):
            build(place(i), part)
            return carry
        lax.fori_loop(1, near_count + 1, one, 0)

    def build_far(part):
        def one(i, carry):
            k = place(i)
            from_cam(PIXELS + part, pixels.at[part], k).wait_recv()
            build(k, part)
            return carry
        lax.fori_loop(near_count + 1, cam_count, one, 0)

    pass_pixels(0)
    build_near(0)
    for j in range(1, opposite):
        pass_grads(j, 0)
    pass_pixels(1)
    build_near(1)
    for j in range(1, opposite):
        pass_grads(j, 1)
    build_far(0)

    from_nodes(VISIBLE, visible_recv).wait_recv()
    unpack(square, visible_recv)
    high, low = split(jnp.transpose(square[...])[0:rows, 0:keys])
    table[0:rows] = high
    table[rows:2 * rows] = low

    piece_tile = tiles[1]

    def project(places, part):
        def awaited(k):
            @pl.when(jnp.logical_and(k != 0, jnp.where(half == 0, k <= opposite, k >= opposite)))
            def _():
                from_cam(GRADS + part, grad_rows.at[part], k).wait_recv()

        def send(k):
            @pl.when(k != 0)
            def _():
                to_cam(PARTIAL + part, partial.at[part, k], partial_recv.at[part], k).start()

        for k in places:
            awaited(k)

        def one(i, carry):
            here = pl.ds(pl.multiple_of(i * piece_tile, piece_tile), piece_tile)
            at = pl.ds(pl.multiple_of(part * part_count + i * piece_tile, piece_tile), piece_tile)
            for k in places:
                picked = dot(table[...], one_hot[k, :, at], ((1,), (0,)))
                g = grad_rows[part, k, :, here]
                summed = jnp.zeros((span, piece_tile), jnp.float32)
                for f in range(per_group):
                    piece = picked[f * span:(f + 1) * span] + picked[rows + f * span:rows + (f + 1) * span]
                    summed = summed + piece * g[f:f + 1]
                partial[part, k, :, here] = jnp.sum(summed * weight[k, :, at], axis=0, keepdims=True)
            return carry
        lax.fori_loop(0, part_count // piece_tile, one, 0)
        for k in places:
            send(k)

    def sum_up(part):
        partial_recv[part, 0] = partial[part, 0]
        from_cams(PARTIAL + part, partial_recv.at[part]).wait_recv()
        summed = partial_recv[part, 0]
        for k in range(1, cam_count):
            summed = summed + partial_recv[part, k]
        total[part, 0] = summed
        for k in near_first[::-1]:
            to_cam_own(TOTAL + part, total.at[part, 0], total.at[part], k).start()

    def give_back(places, part):
        def awaited(k):
            @pl.when(k != 0)
            def _():
                from_cam(TOTAL + part, total.at[part], k).wait_recv()

        for k in places:
            awaited(k)

        def one(i, carry):
            here = pl.ds(pl.multiple_of(i * piece_tile, piece_tile), piece_tile)
            at = pl.ds(pl.multiple_of(part * part_count + i * piece_tile, piece_tile), piece_tile)
            summed = returned[...]
            for k in places:
                scaled = grad_rows[part, k, :, here] * total[part, k, :, here]
                w = weight[k, :, at]
                products = jnp.concatenate([w * scaled[f:f + 1] for f in range(per_group)], axis=0)
                high, low = split(products)
                both = jnp.concatenate([high, low], axis=0)
                summed = summed + dot(both, one_hot[k, :, at], ((1,), (1,)))
            returned[...] = summed
            return carry
        lax.fori_loop(0, part_count // piece_tile, one, 0)

    def listed(i, places):
        k = jnp.int32(places[0])
        for at, which in enumerate(places):
            k = jnp.where(i == at, which, k)
        return k

    out_order = near_first[::-1] + [0]
    back_order = [0] + near_first

    def project_some(start, stop, part):
        def one(i, carry):
            project([listed(i, out_order[at::QUAD]) for at in range(QUAD)], part)
            return carry
        lax.fori_loop(start, stop, one, 0)

    def give_back_some(start, stop, part):
        def one(i, carry):
            give_back([listed(i, back_order[0::2]), listed(i, back_order[1::2])], part)
            return carry
        lax.fori_loop(start, stop, one, 0)

    pairs_count = cam_count // 2
    project_some(0, cam_count // QUAD, 0)
    build_far(1)
    project_some(0, cam_count // QUAD, 1)
    sum_up(0)
    returned[...] = jnp.zeros_like(returned)
    to_frame(0).wait_recv()
    to_frame(1).wait_recv()
    ids = lax.broadcasted_iota(jnp.int32, (width, width), 0)
    lanes = lax.broadcasted_iota(jnp.int32, (width, width), 1)
    identity = jnp.where(ids == lanes, 1.0, 0.0)
    has_earlier = jnp.where(me_node >= frame_step, 1.0, 0.0)
    has_following = jnp.where(me_node < node_count - frame_step, 1.0, 0.0)
    for q in range(local):
        edges = jnp.concatenate(
            [identity - jnp.where(ids == rigid_nbr[r, q:q + 1, :], 1.0, 0.0) for r in range(rigid_nbr.shape[0])], axis=1
        ).astype(jnp.bfloat16)
        patch = jnp.concatenate([direction[f, q:q + 1, :] for f in range(params)], axis=0)
        high, low = split(patch)
        difference = dot(high, edges, ((1,), (0,))) + dot(low, edges, ((1,), (0,)))
        high, low = split(difference)
        rigid = dot(high, edges, ((1,), (1,))) + dot(low, edges, ((1,), (1,)))
        for f in range(params):
            here = direction[f, q:q + 1, :]
            time = 2.0 * here - has_earlier * frame_recv[0, f, q:q + 1, :] - has_following * frame_recv[1, f, q:q + 1, :]
            rest_send[f // per_group, 2, f % per_group, q:q + 1, :] = rigid_weight * rigid[f:f + 1] + temporal_weight * time
    rest_recv[0] = rest_send[group]


    each_cam(lambda k: to_cam(REST, rest_send.at[peer_group(k)], rest_recv, k).start())
    sum_up(1)
    give_back_some(0, pairs_count, 0)
    give_back_some(0, pairs_count, 1)
    square[...] = jnp.zeros_like(square)
    square[0:rows, 0:keys] = returned[0:rows] + returned[rows:2 * rows]
    by_key = jnp.transpose(square[...])
    pack(returns_send, by_key)
    returns_recv[pl.ds(me_node, 1)] = returns_send[pl.ds(me_node, 1)]
    send_nodes(RETURNS, returns_send, returns_recv)

    start_norm = jnp.sum(residual[...] * precond[...] * residual[...], axis=(0, 1))[None]
    from_cams(REST, rest_recv).wait_recv()
    for which, target in enumerate((owned_resid, owned_prec, owned_smooth)):
        gather_owned(rest_recv, target, which)
    mine = halves(owned)
    mine_prec = halves(owned_prec)
    weighted_resid = halves(owned_resid) * mine_prec

    from_nodes(RETURNS, returns_recv).wait_recv()
    pieces = halves(owned_smooth)
    unpack(square, returns_recv)
    one_hot_rows = chosen[...].astype(jnp.bfloat16)
    high, low = split(square[0:keys, 0:rows])
    pieces = pieces + dot(one_hot_rows, high, ((1,), (0,))) + dot(one_hot_rows, low, ((1,), (0,)))

    lane = lax.broadcasted_iota(jnp.int32, (1, width), 1)

    def spread(value, which):
        return jnp.where(lane == which, jnp.sum(value), 0.0)

    mine_sums = (
        spread(start_norm, 0) + spread(mine * pieces, 1) + spread(weighted_resid * pieces, 2)
        + spread(mine_prec * pieces * pieces, 3)
    )
    node_sums[pl.ds(me_node, 1)] = mine_sums[None]
    send_nodes(NODE_SUMS, node_sums, node_sums, indexed=False)

    for f in range(per_group):
        piece = pieces[:, f * span:(f + 1) * span]
        doubled = jnp.concatenate([piece, piece], axis=1)
        for k in range(cam_count):
            image_send[k, f] = doubled[k * local:(k + 1) * local]
    image_recv[0] = image_send[0]
    each_cam(lambda k: to_cam(IMAGE, image_send.at[k], image_recv, k).start())

    from_nodes(NODE_SUMS, node_sums).wait_recv()
    cam_send[0] = jnp.sum(node_sums[...], axis=0)
    cam_sums[0] = cam_send[0]
    each_cam(lambda k: to_cam(SUMS, cam_send.at[0], cam_sums, k).start())

    from_cams(IMAGE, image_recv).wait_recv()
    lane2 = lax.broadcasted_iota(jnp.int32, (local, width), 1)
    for g in range(params // per_group):
        for f in range(per_group):
            sides = [
                image_recv[lax.rem(HALVES * g + s + cam_count - me_cam, cam_count), f] for s in range(HALVES)
            ]
            image[g * per_group + f] = jnp.where(lane2 < span, sides[0], sides[1])

    from_cams(SUMS, cam_sums).wait_recv()
    sums = jnp.sum(cam_sums[...], axis=0)

    def value_of(which):
        return jnp.sum(jnp.where(lane == which, sums, 0.0), axis=1, keepdims=True)

    start, curvature, cross, square_norm = (value_of(which) for which in range(4))
    step = start / curvature
    new_norm = start - 2.0 * step * cross + step * step * square_norm
    ratio = new_norm / start
    for f in range(params):
        left = residual[f] - step * image[f]
        result[f] = iterate[f] + step * direction[f]
        result[params + f] = left
        result[2 * params + f] = precond[f] * left + ratio * direction[f]

    for phase, target in (
        (OWNED, owned_recv), (REST, rest_recv),
        (IMAGE, image_recv), (SUMS, cam_sums),
    ):
        from_cams(phase, target).wait_send()
    for part in range(PARTS):
        from_cams(PIXELS + part, pixels.at[part]).wait_send()
        from_cams(GRADS + part, grad_rows.at[part]).wait_send()
        from_cams(TOTAL + part, total.at[part]).wait_send()
        from_cams(PARTIAL + part, partial_recv.at[part]).wait_send()
    to_frame(0).wait_send()
    to_frame(1).wait_send()
    for phase, target in ((VISIBLE, visible_recv), (RETURNS, returns_recv), (NODE_SUMS, node_sums)):
        from_nodes(phase, target).wait_send()


def solution(mesh):
    node_count, cam_count = mesh.shape["nodes"], mesh.shape["cams"]

    def on_device(iterate, residual, direction, precond, send_list, grads, node_refs, skin, rigid_nbr):
        local, params, width = direction.shape
        pixel_count = node_refs.shape[1]
        slots = send_list.shape[2]
        groups = cam_count // HALVES
        per_group = params // groups
        span = width // HALVES
        rows = per_group * span
        held = local * cam_count
        keys = slots * node_count
        part_count = pixel_count // PARTS
        tiles = tuple(min(size, part_count) for size in TILES)
        up = lambda size, to: (size + to - 1) // to * to
        side = up(max(rows, keys), 128)
        message = slots * (per_group // 2) + (per_group % 2) * ((slots + 1) // 2)
        turn = lambda value: jnp.transpose(value, (1, 0, 2))
        f32, bf16 = jnp.float32, jnp.bfloat16
        slice_shape = (cam_count, per_group, local, width)
        dma = pltpu.SemaphoreType.DMA
        vmem = pl.BlockSpec(memory_space=pltpu.VMEM)
        inputs = (
            turn(iterate), turn(residual), turn(direction), turn(precond), jnp.transpose(send_list, (2, 0, 1)),
            grads, node_refs, skin, turn(rigid_nbr),
        )
        result = pl.pallas_call(
            functools.partial(kernel, node_count, cam_count, tiles),
            out_shape=jax.ShapeDtypeStruct((3 * params, local, width), f32),
            in_specs=[pl.BlockSpec(memory_space=pl.ANY)] * 9,
            out_specs=vmem,
            scratch_shapes=[
                *(pltpu.VMEM(value.shape, value.dtype) for value in inputs),
                pltpu.VMEM((PARTS, cam_count, 8, part_count), f32),
                pltpu.VMEM((PARTS, groups, per_group, part_count), f32),
                pltpu.VMEM((PARTS, cam_count, per_group, part_count), f32),
                pltpu.VMEM((cam_count, keys, pixel_count), bf16),
                pltpu.VMEM((cam_count, span, pixel_count), f32),
                pltpu.VMEM(slice_shape, f32),
                pltpu.VMEM((groups, 3, per_group, local, width), f32),
                pltpu.VMEM((cam_count, 3, per_group, local, width), f32),
                pltpu.VMEM((2, params, local, width), f32),
                pltpu.VMEM((per_group, held, width), f32),
                pltpu.VMEM((per_group, held, width), f32),
                pltpu.VMEM((per_group, held, width), f32),
                pltpu.VMEM((per_group, held, width), f32),
                pltpu.VMEM((held, keys), f32),
                pltpu.VMEM((node_count, message, width), f32),
                pltpu.VMEM((node_count, message, width), f32),
                pltpu.VMEM((2 * rows, keys), bf16),
                pltpu.VMEM((PARTS, cam_count, 1, part_count), f32),
                pltpu.VMEM((PARTS, cam_count, 1, part_count), f32),
                pltpu.VMEM((PARTS, cam_count, 1, part_count), f32),
                pltpu.VMEM((2 * rows, keys), f32),
                pltpu.VMEM((side, side), f32),
                pltpu.VMEM((node_count, message, width), f32),
                pltpu.VMEM((node_count, message, width), f32),
                pltpu.VMEM(slice_shape, f32),
                pltpu.VMEM(slice_shape, f32),
                pltpu.VMEM((params, local, width), f32),
                pltpu.VMEM((node_count, 1, width), f32),
                pltpu.VMEM((cam_count, 1, width), f32),
                pltpu.VMEM((1, 1, width), f32),
                dma((12,)),
                dma((12,)),
                dma((6, cam_count)),
                dma((3,)),
                dma((3,)),
                dma((2,)),
                dma((2,)),
                dma((9,)),
            ],
            compiler_params=pltpu.CompilerParams(collective_id=0, has_side_effects=True, vmem_limit_bytes=60 << 20),
            name="cg_step",
        )(*inputs)
        return tuple(turn(result[i * params:(i + 1) * params]) for i in range(3))

    spec = P(("nodes", "cams"), None, None)
    split_last = P(None, ("nodes", "cams"))
    return jax.shard_map(
        on_device,
        mesh=mesh,
        in_specs=(spec, spec, spec, spec, P("nodes", None, None), split_last, split_last, split_last, spec),
        out_specs=(spec, spec, spec),
        check_vma=False,
    )
```

```python
import functools

import jax
import jax.numpy as jnp
from jax import lax
from jax.experimental import pallas as pl
from jax.experimental.pallas import tpu as pltpu
from jax.sharding import PartitionSpec as P

MESH = pl.DeviceIdType.MESH
FRAMES = 8
REACH = 2
TILES = (512, 1024)
PARTS = 2
QUAD = 4
HALVES = 2
temporal_weight = 0.5
rigid_weight = 0.1

PIXELS, PIXELS_B, GRADS, GRADS_B, TOTAL, TOTAL_B, OWNED, REST, PARTIAL, PARTIAL_B, IMAGE, SUMS = range(12)
VISIBLE, RETURNS, NODE_SUMS = range(3)


def split(value):
    high = value.astype(jnp.bfloat16)
    return high, (value - high.astype(jnp.float32)).astype(jnp.bfloat16)


def dot(left, right, contract):
    return lax.dot_general(left, right, (contract, ((), ())), preferred_element_type=jnp.float32)


def kernel(
    node_count, cam_count, tiles,
    iterate_in, residual_in, direction_in, precond_in, send_list_in, grads_in, node_refs_in, skin_in, rigid_nbr_in,
    result,
    iterate, residual, direction, precond, send_list, grads, node_refs, skin, rigid_nbr,
    pixels, grad_send, grad_rows, one_hot, weight,
    owned_recv, rest_send, rest_recv, frame_recv,
    owned, owned_resid, owned_prec, owned_smooth,
    chosen, visible_send, visible_recv, table, partial, partial_recv, total, returned, square,
    returns_send, returns_recv, image_send, image_recv, image,
    node_sums, cam_sums, cam_send,
    cam_send_sem, cam_recv_sem, slot_sem, node_send_sem, node_recv_sem, frame_send_sem, frame_recv_sem, input_sem,
):
    me_node = lax.axis_index("nodes")
    me_cam = lax.axis_index("cams")
    group = me_cam // HALVES
    half = lax.rem(me_cam, HALVES)
    params, local, width = direction.shape
    slots = send_list.shape[0]
    per_group = grad_send.shape[2]
    span = width // HALVES
    rows = per_group * span
    keys = slots * node_count
    pixel_count = node_refs.shape[1]
    held = local * cam_count
    first = group * per_group
    frame_step = node_count // FRAMES

    pairs = (
        (node_refs_in, node_refs), (skin_in, skin), (grads_in, grads), (direction_in, direction),
        (residual_in, residual), (precond_in, precond), (send_list_in, send_list), (rigid_nbr_in, rigid_nbr),
        (iterate_in, iterate),
    )
    inputs = [pltpu.make_async_copy(source, target, input_sem.at[i]) for i, (source, target) in enumerate(pairs)]
    barrier = pltpu.get_barrier_semaphore()

    def wrap(value, size):
        return jnp.where(value >= size, value - size, value)

    def each_node(body):
        middle = node_count // 2
        body(middle)

        def both(i, carry):
            body(middle + i)
            body(middle - i)
            return carry

        lax.fori_loop(1, middle, both, 0)

    def cam_peer(k):
        return wrap(me_cam + k, cam_count)

    cam_peers = [me_cam] + [wrap(me_cam + k, cam_count) for k in range(1, cam_count)]
    near_first = [k for d in range(1, cam_count // 2 + 1) for k in sorted({d, cam_count - d})]

    def place(i):
        return jnp.where(lax.rem(i, 2) == 1, (i + 1) // 2, cam_count - i // 2)

    def each_cam(body):
        for k in near_first:
            body(k)

    def greet(**place):
        pl.semaphore_signal(barrier, inc=1, device_id=place, device_id_type=MESH)

    each_cam(lambda k: greet(cams=cam_peers[k]))
    for copy in inputs:
        copy.start()
    each_node(lambda k: greet(nodes=wrap(me_node + k, node_count)))

    def to_cam(phase, source, target, k):
        slot = cam_count - k
        return pltpu.make_async_remote_copy(
            src_ref=source, dst_ref=target.at[slot],
            send_sem=cam_send_sem.at[phase], recv_sem=cam_recv_sem.at[phase],
            device_id={"cams": cam_peer(k)}, device_id_type=MESH,
        )

    def from_cams(phase, target):
        return pltpu.make_async_remote_copy(
            src_ref=target.at[pl.ds(1, cam_count - 1)], dst_ref=target.at[pl.ds(1, cam_count - 1)],
            send_sem=cam_send_sem.at[phase], recv_sem=cam_recv_sem.at[phase],
            device_id={"cams": cam_peers[1]}, device_id_type=MESH,
        )

    def to_cam_slot(phase, source, target, k, slot):
        return pltpu.make_async_remote_copy(
            src_ref=source, dst_ref=target.at[slot],
            send_sem=cam_send_sem.at[phase], recv_sem=slot_sem.at[phase, slot],
            device_id={"cams": cam_peer(k)}, device_id_type=MESH,
        )

    def to_cam_own(phase, source, target, k):
        return to_cam_slot(phase, source, target, k, cam_count - k)

    def from_cam(phase, target, k):
        return pltpu.make_async_remote_copy(
            src_ref=target.at[k], dst_ref=target.at[k],
            send_sem=cam_send_sem.at[phase], recv_sem=slot_sem.at[phase, k],
            device_id={"cams": cam_peer(k)}, device_id_type=MESH,
        )

    def to_node(phase, source, target, k, indexed):
        peer = wrap(me_node + k, node_count)
        return pltpu.make_async_remote_copy(
            src_ref=source.at[peer] if indexed else source.at[me_node], dst_ref=target.at[me_node],
            send_sem=node_send_sem.at[phase], recv_sem=node_recv_sem.at[phase],
            device_id={"nodes": peer}, device_id_type=MESH,
        )

    def from_nodes(phase, target):
        return pltpu.make_async_remote_copy(
            src_ref=target.at[pl.ds(0, node_count - 1)], dst_ref=target.at[pl.ds(0, node_count - 1)],
            send_sem=node_send_sem.at[phase], recv_sem=node_recv_sem.at[phase],
            device_id={"nodes": lax.rem(me_node + 1, node_count)}, device_id_type=MESH,
        )

    def send_nodes(phase, source, target, indexed=True):
        each_node(lambda k: to_node(phase, source, target, k, indexed).start())

    for copy in inputs:
        copy.wait()
    part_count = pixel_count // PARTS
    grad_all = grads[...].astype(jnp.float32)
    for part in range(PARTS):
        columns = slice(part * part_count, (part + 1) * part_count)
        pixels[part, 0, 0:4, :] = node_refs[:, columns].astype(jnp.float32)
        pixels[part, 0, 4:8, :] = skin[:, columns].astype(jnp.float32)
        for g in range(params // per_group):
            grad_send[part, g] = grad_all[g * per_group:(g + 1) * per_group, columns]
        grad_rows[part, 0] = grad_send[part, group]
    for g in range(params // per_group):
        rest_send[g, 0] = residual[g * per_group:(g + 1) * per_group]
        rest_send[g, 1] = precond[g * per_group:(g + 1) * per_group]
    owned_recv[0] = direction[pl.ds(first, per_group)]

    pl.semaphore_wait(barrier, cam_count - 1 + node_count - 1)

    def peer_group(k):
        return cam_peers[k] // HALVES

    def peer_params(source, k):
        return source.at[pl.ds(peer_group(k) * per_group, per_group)]

    each_cam(lambda k: to_cam(OWNED, peer_params(direction, k), owned_recv, k).start())

    def to_frame(which):
        by = frame_step if which == 0 else node_count - frame_step
        return pltpu.make_async_remote_copy(
            src_ref=direction, dst_ref=frame_recv.at[which],
            send_sem=frame_send_sem.at[which], recv_sem=frame_recv_sem.at[which],
            device_id={"nodes": lax.rem(me_node + by, node_count)}, device_id_type=MESH,
        )

    to_frame(0).start()
    to_frame(1).start()

    opposite = cam_count // 2
    ring = [d for step in range(1, opposite + 1) for d in ((step, -step) if step < opposite else (step,))]

    def place_of(distance):
        return distance % cam_count

    def side(distance):
        return jnp.where(half == 0, distance % cam_count, -distance % cam_count)

    def arrive(distance, part):
        from_cam(PIXELS + part, pixels.at[part], place_of(distance)).wait_recv()
        on = distance + (1 if distance > 0 else -1)
        if abs(distance) == REACH and abs(on) < opposite:
            to_cam_slot(
                PIXELS + part, pixels.at[part, place_of(distance)], pixels.at[part], place_of(distance - on), place_of(on)
            ).start()

    def pass_opposite(part):
        if REACH < opposite:
            have = side(REACH)
            to_cam_slot(PIXELS + part, pixels.at[part, have], pixels.at[part], side(REACH - opposite), opposite).start()

    def send_grads(distance, part):
        k = side(distance)
        source = grad_send.at[part, cam_peer(k) // HALVES]
        to_cam_slot(GRADS + part, source, grad_rows.at[part], k, side(-distance)).start()

    def pass_grads(distance, part):
        have = side(-distance)
        from_cam(GRADS + part, grad_rows.at[part], have).wait_recv()
        to_cam_slot(GRADS + part, grad_rows.at[part, have], grad_rows.at[part], side(1), side(-distance - 1)).start()

    def send_pixels(part):
        for d in ring[::-1]:
            if abs(d) <= REACH:
                to_cam_slot(PIXELS + part, pixels.at[part, 0], pixels.at[part], place_of(-d), place_of(d)).start()
        for j in range(opposite - 1, 0, -1):
            send_grads(j if j % 2 == 0 else -j, part)
        send_grads(1, part)

    near_ring = [d for d in ring if abs(d) <= REACH]

    def pass_pixels(part):
        for d in near_ring[::-1]:
            arrive(d, part)
            if d == REACH:
                pass_opposite(part)

    send_pixels(0)
    send_pixels(1)

    tile = tiles[0]

    def build(k, part):
        def one(i, carry):
            here = pl.ds(pl.multiple_of(i * tile, tile), tile)
            at = pl.ds(pl.multiple_of(part * part_count + i * tile, tile), tile)
            block = pixels[part, k, :, here]
            refs = block[0:4].astype(jnp.int32)
            weights = block[4:8]
            place = refs[0:1] >> 7
            source = (place * 171) >> 9
            key = (place - slots * source) * node_count + source
            hits = lax.broadcasted_iota(jnp.int32, (keys, tile), 0) == key
            one_hot[k, :, at] = jnp.where(hits, 1.0, 0.0).astype(jnp.bfloat16)
            within = (refs & (width - 1)) - half * span
            ids = lax.broadcasted_iota(jnp.int32, (span, tile), 0)
            summed = jnp.zeros((span, tile), jnp.float32)
            for s in range(4):
                summed = summed + jnp.where(ids == within[s:s + 1], weights[s:s + 1], 0.0)
            weight[k, :, at] = summed
            return carry
        lax.fori_loop(0, part_count // tile, one, 0)

    for part in range(PARTS):
        build(0, part)

    wanted = lax.broadcasted_iota(jnp.int32, (held, node_count), 0)
    for j in range(slots):
        listed = send_list[j]
        shifted = lax.rem(listed // local + cam_count - me_cam, cam_count) * local + lax.rem(listed, local)
        shifted = jnp.where(listed >= 0, shifted, -1)
        chosen[:, j * node_count:(j + 1) * node_count] = jnp.where(wanted == shifted, 1.0, 0.0)

    def take_half(value):
        return jnp.where(half == 0, value[:, :span], value[:, span:])

    def gather_owned(received, target, *which):
        for k in range(cam_count):
            for f in range(per_group):
                target[f, k * local:(k + 1) * local, :] = received[(k, *which, f)]

    def halves(target):
        return jnp.concatenate([take_half(target[f]) for f in range(per_group)], axis=1)

    whole, odd = per_group // 2, per_group % 2

    def pack(target, value):
        for j in range(slots):
            part = value[j * node_count:(j + 1) * node_count]
            for p in range(whole):
                target[:, j * whole + p, :] = part[:, p * width:(p + 1) * width]
        if odd:
            at = whole * width
            last = [value[j * node_count:(j + 1) * node_count, at:at + span] for j in range(slots)]
            last = last + [jnp.zeros_like(last[0])] * (slots % 2)
            for i in range(0, slots, 2):
                target[:, slots * whole + i // 2, :] = jnp.concatenate(last[i:i + 2], axis=1)

    def unpack(target, source):
        for j in range(slots):
            at = pl.ds(j * node_count, node_count)
            for p in range(whole):
                target[at, p * width:(p + 1) * width] = source[:, j * whole + p, :]
            if odd:
                pair = source[:, slots * whole + j // 2, :]
                side = span * (j % 2)
                target[at, whole * width:whole * width + span] = pair[:, side:side + span]

    from_cams(OWNED, owned_recv).wait_recv()
    gather_owned(owned_recv, owned)
    mine = halves(owned)
    one_hot_rows = chosen[...].astype(jnp.bfloat16)
    high, low = split(mine)
    listed_rows = dot(one_hot_rows, high, ((0,), (0,))) + dot(one_hot_rows, low, ((0,), (0,)))
    pack(visible_send, listed_rows)
    visible_recv[pl.ds(me_node, 1)] = visible_send[pl.ds(me_node, 1)]
    send_nodes(VISIBLE, visible_send, visible_recv)

    near_count = len(near_ring)

    def build_near(part):
        def one(i, carry):
            build(place(i), part)
            return carry
        lax.fori_loop(1, near_count + 1, one, 0)

    def build_far(part):
        def one(i, carry):
            k = place(i)
            from_cam(PIXELS + part, pixels.at[part], k).wait_recv()
            build(k, part)
            return carry
        lax.fori_loop(near_count + 1, cam_count, one, 0)

    pass_pixels(0)
    build_near(0)
    for j in range(1, opposite):
        pass_grads(j, 0)
    pass_pixels(1)
    build_near(1)
    for j in range(1, opposite):
        pass_grads(j, 1)
    build_far(0)

    from_nodes(VISIBLE, visible_recv).wait_recv()
    unpack(square, visible_recv)
    high, low = split(jnp.transpose(square[...])[0:rows, 0:keys])
    table[0:rows] = high
    table[rows:2 * rows] = low

    piece_tile = tiles[1]

    def project(places, part):
        def awaited(k):
            @pl.when(jnp.logical_and(k != 0, jnp.where(half == 0, k <= opposite, k >= opposite)))
            def _():
                from_cam(GRADS + part, grad_rows.at[part], k).wait_recv()

        def send(k):
            @pl.when(k != 0)
            def _():
                to_cam(PARTIAL + part, partial.at[part, k], partial_recv.at[part], k).start()

        for k in places:
            awaited(k)

        def one(i, carry):
            here = pl.ds(pl.multiple_of(i * piece_tile, piece_tile), piece_tile)
            at = pl.ds(pl.multiple_of(part * part_count + i * piece_tile, piece_tile), piece_tile)
            for k in places:
                picked = dot(table[...], one_hot[k, :, at], ((1,), (0,)))
                g = grad_rows[part, k, :, here]
                summed = jnp.zeros((span, piece_tile), jnp.float32)
                for f in range(per_group):
                    piece = picked[f * span:(f + 1) * span] + picked[rows + f * span:rows + (f + 1) * span]
                    summed = summed + piece * g[f:f + 1]
                partial[part, k, :, here] = jnp.sum(summed * weight[k, :, at], axis=0, keepdims=True)
            return carry
        lax.fori_loop(0, part_count // piece_tile, one, 0)
        for k in places:
            send(k)

    def sum_up(part):
        partial_recv[part, 0] = partial[part, 0]
        from_cams(PARTIAL + part, partial_recv.at[part]).wait_recv()
        summed = partial_recv[part, 0]
        for k in range(1, cam_count):
            summed = summed + partial_recv[part, k]
        total[part, 0] = summed
        for k in near_first[::-1]:
            to_cam_own(TOTAL + part, total.at[part, 0], total.at[part], k).start()

    def give_back(places, part):
        def awaited(k):
            @pl.when(k != 0)
            def _():
                from_cam(TOTAL + part, total.at[part], k).wait_recv()

        for k in places:
            awaited(k)

        def one(i, carry):
            here = pl.ds(pl.multiple_of(i * piece_tile, piece_tile), piece_tile)
            at = pl.ds(pl.multiple_of(part * part_count + i * piece_tile, piece_tile), piece_tile)
            summed = returned[...]
            for k in places:
                scaled = grad_rows[part, k, :, here] * total[part, k, :, here]
                w = weight[k, :, at]
                products = jnp.concatenate([w * scaled[f:f + 1] for f in range(per_group)], axis=0)
                high, low = split(products)
                both = jnp.concatenate([high, low], axis=0)
                summed = summed + dot(both, one_hot[k, :, at], ((1,), (1,)))
            returned[...] = summed
            return carry
        lax.fori_loop(0, part_count // piece_tile, one, 0)

    def listed(i, places):
        k = jnp.int32(places[0])
        for at, which in enumerate(places):
            k = jnp.where(i == at, which, k)
        return k

    out_order = near_first[::-1] + [0]
    back_order = [0] + near_first

    def project_some(start, stop, part):
        def one(i, carry):
            project([listed(i, out_order[at::QUAD]) for at in range(QUAD)], part)
            return carry
        lax.fori_loop(start, stop, one, 0)

    def give_back_some(start, stop, part):
        def one(i, carry):
            give_back([listed(i, back_order[at::QUAD]) for at in range(QUAD)], part)
            return carry
        lax.fori_loop(start, stop, one, 0)

    project_some(0, cam_count // QUAD, 0)
    build_far(1)
    project_some(0, cam_count // QUAD, 1)
    sum_up(0)
    returned[...] = jnp.zeros_like(returned)
    to_frame(0).wait_recv()
    to_frame(1).wait_recv()
    ids = lax.broadcasted_iota(jnp.int32, (width, width), 0)
    lanes = lax.broadcasted_iota(jnp.int32, (width, width), 1)
    identity = jnp.where(ids == lanes, 1.0, 0.0)
    has_earlier = jnp.where(me_node >= frame_step, 1.0, 0.0)
    has_following = jnp.where(me_node < node_count - frame_step, 1.0, 0.0)
    for q in range(local):
        edges = jnp.concatenate(
            [identity - jnp.where(ids == rigid_nbr[r, q:q + 1, :], 1.0, 0.0) for r in range(rigid_nbr.shape[0])], axis=1
        ).astype(jnp.bfloat16)
        patch = jnp.concatenate([direction[f, q:q + 1, :] for f in range(params)], axis=0)
        high, low = split(patch)
        difference = dot(high, edges, ((1,), (0,))) + dot(low, edges, ((1,), (0,)))
        high, low = split(difference)
        rigid = dot(high, edges, ((1,), (1,))) + dot(low, edges, ((1,), (1,)))
        for f in range(params):
            here = direction[f, q:q + 1, :]
            time = 2.0 * here - has_earlier * frame_recv[0, f, q:q + 1, :] - has_following * frame_recv[1, f, q:q + 1, :]
            rest_send[f // per_group, 2, f % per_group, q:q + 1, :] = rigid_weight * rigid[f:f + 1] + temporal_weight * time
    rest_recv[0] = rest_send[group]


    each_cam(lambda k: to_cam(REST, rest_send.at[peer_group(k)], rest_recv, k).start())
    sum_up(1)
    give_back_some(0, cam_count // QUAD, 0)
    give_back_some(0, cam_count // QUAD, 1)
    square[...] = jnp.zeros_like(square)
    square[0:rows, 0:keys] = returned[0:rows] + returned[rows:2 * rows]
    by_key = jnp.transpose(square[...])
    pack(returns_send, by_key)
    returns_recv[pl.ds(me_node, 1)] = returns_send[pl.ds(me_node, 1)]
    send_nodes(RETURNS, returns_send, returns_recv)

    start_norm = jnp.sum(residual[...] * precond[...] * residual[...], axis=(0, 1))[None]
    from_cams(REST, rest_recv).wait_recv()
    for which, target in enumerate((owned_resid, owned_prec, owned_smooth)):
        gather_owned(rest_recv, target, which)
    mine = halves(owned)
    mine_prec = halves(owned_prec)
    weighted_resid = halves(owned_resid) * mine_prec

    from_nodes(RETURNS, returns_recv).wait_recv()
    pieces = halves(owned_smooth)
    unpack(square, returns_recv)
    one_hot_rows = chosen[...].astype(jnp.bfloat16)
    high, low = split(square[0:keys, 0:rows])
    pieces = pieces + dot(one_hot_rows, high, ((1,), (0,))) + dot(one_hot_rows, low, ((1,), (0,)))

    lane = lax.broadcasted_iota(jnp.int32, (1, width), 1)

    def spread(value, which):
        return jnp.where(lane == which, jnp.sum(value), 0.0)

    mine_sums = (
        spread(start_norm, 0) + spread(mine * pieces, 1) + spread(weighted_resid * pieces, 2)
        + spread(mine_prec * pieces * pieces, 3)
    )
    node_sums[pl.ds(me_node, 1)] = mine_sums[None]
    send_nodes(NODE_SUMS, node_sums, node_sums, indexed=False)

    for f in range(per_group):
        piece = pieces[:, f * span:(f + 1) * span]
        doubled = jnp.concatenate([piece, piece], axis=1)
        for k in range(cam_count):
            image_send[k, f] = doubled[k * local:(k + 1) * local]
    image_recv[0] = image_send[0]
    each_cam(lambda k: to_cam(IMAGE, image_send.at[k], image_recv, k).start())

    from_nodes(NODE_SUMS, node_sums).wait_recv()
    cam_send[0] = jnp.sum(node_sums[...], axis=0)
    cam_sums[0] = cam_send[0]
    each_cam(lambda k: to_cam(SUMS, cam_send.at[0], cam_sums, k).start())

    from_cams(IMAGE, image_recv).wait_recv()
    lane2 = lax.broadcasted_iota(jnp.int32, (local, width), 1)
    for g in range(params // per_group):
        for f in range(per_group):
            sides = [
                image_recv[lax.rem(HALVES * g + s + cam_count - me_cam, cam_count), f] for s in range(HALVES)
            ]
            image[g * per_group + f] = jnp.where(lane2 < span, sides[0], sides[1])

    from_cams(SUMS, cam_sums).wait_recv()
    sums = jnp.sum(cam_sums[...], axis=0)

    def value_of(which):
        return jnp.sum(jnp.where(lane == which, sums, 0.0), axis=1, keepdims=True)

    start, curvature, cross, square_norm = (value_of(which) for which in range(4))
    step = start / curvature
    new_norm = start - 2.0 * step * cross + step * step * square_norm
    ratio = new_norm / start
    for f in range(params):
        left = residual[f] - step * image[f]
        result[f] = iterate[f] + step * direction[f]
        result[params + f] = left
        result[2 * params + f] = precond[f] * left + ratio * direction[f]

    for phase, target in (
        (OWNED, owned_recv), (REST, rest_recv),
        (IMAGE, image_recv), (SUMS, cam_sums),
    ):
        from_cams(phase, target).wait_send()
    for part in range(PARTS):
        from_cams(PIXELS + part, pixels.at[part]).wait_send()
        from_cams(GRADS + part, grad_rows.at[part]).wait_send()
        from_cams(TOTAL + part, total.at[part]).wait_send()
        from_cams(PARTIAL + part, partial_recv.at[part]).wait_send()
    to_frame(0).wait_send()
    to_frame(1).wait_send()
    for phase, target in ((VISIBLE, visible_recv), (RETURNS, returns_recv), (NODE_SUMS, node_sums)):
        from_nodes(phase, target).wait_send()


def solution(mesh):
    node_count, cam_count = mesh.shape["nodes"], mesh.shape["cams"]

    def on_device(iterate, residual, direction, precond, send_list, grads, node_refs, skin, rigid_nbr):
        local, params, width = direction.shape
        pixel_count = node_refs.shape[1]
        slots = send_list.shape[2]
        groups = cam_count // HALVES
        per_group = params // groups
        span = width // HALVES
        rows = per_group * span
        held = local * cam_count
        keys = slots * node_count
        part_count = pixel_count // PARTS
        tiles = tuple(min(size, part_count) for size in TILES)
        up = lambda size, to: (size + to - 1) // to * to
        side = up(max(rows, keys), 128)
        message = slots * (per_group // 2) + (per_group % 2) * ((slots + 1) // 2)
        turn = lambda value: jnp.transpose(value, (1, 0, 2))
        f32, bf16 = jnp.float32, jnp.bfloat16
        slice_shape = (cam_count, per_group, local, width)
        dma = pltpu.SemaphoreType.DMA
        vmem = pl.BlockSpec(memory_space=pltpu.VMEM)
        inputs = (
            turn(iterate), turn(residual), turn(direction), turn(precond), jnp.transpose(send_list, (2, 0, 1)),
            grads, node_refs, skin, turn(rigid_nbr),
        )
        result = pl.pallas_call(
            functools.partial(kernel, node_count, cam_count, tiles),
            out_shape=jax.ShapeDtypeStruct((3 * params, local, width), f32),
            in_specs=[pl.BlockSpec(memory_space=pl.ANY)] * 9,
            out_specs=vmem,
            scratch_shapes=[
                *(pltpu.VMEM(value.shape, value.dtype) for value in inputs),
                pltpu.VMEM((PARTS, cam_count, 8, part_count), f32),
                pltpu.VMEM((PARTS, groups, per_group, part_count), f32),
                pltpu.VMEM((PARTS, cam_count, per_group, part_count), f32),
                pltpu.VMEM((cam_count, keys, pixel_count), bf16),
                pltpu.VMEM((cam_count, span, pixel_count), f32),
                pltpu.VMEM(slice_shape, f32),
                pltpu.VMEM((groups, 3, per_group, local, width), f32),
                pltpu.VMEM((cam_count, 3, per_group, local, width), f32),
                pltpu.VMEM((2, params, local, width), f32),
                pltpu.VMEM((per_group, held, width), f32),
                pltpu.VMEM((per_group, held, width), f32),
                pltpu.VMEM((per_group, held, width), f32),
                pltpu.VMEM((per_group, held, width), f32),
                pltpu.VMEM((held, keys), f32),
                pltpu.VMEM((node_count, message, width), f32),
                pltpu.VMEM((node_count, message, width), f32),
                pltpu.VMEM((2 * rows, keys), bf16),
                pltpu.VMEM((PARTS, cam_count, 1, part_count), f32),
                pltpu.VMEM((PARTS, cam_count, 1, part_count), f32),
                pltpu.VMEM((PARTS, cam_count, 1, part_count), f32),
                pltpu.VMEM((2 * rows, keys), f32),
                pltpu.VMEM((side, side), f32),
                pltpu.VMEM((node_count, message, width), f32),
                pltpu.VMEM((node_count, message, width), f32),
                pltpu.VMEM(slice_shape, f32),
                pltpu.VMEM(slice_shape, f32),
                pltpu.VMEM((params, local, width), f32),
                pltpu.VMEM((node_count, 1, width), f32),
                pltpu.VMEM((cam_count, 1, width), f32),
                pltpu.VMEM((1, 1, width), f32),
                dma((12,)),
                dma((12,)),
                dma((6, cam_count)),
                dma((3,)),
                dma((3,)),
                dma((2,)),
                dma((2,)),
                dma((9,)),
            ],
            compiler_params=pltpu.CompilerParams(collective_id=0, has_side_effects=True, vmem_limit_bytes=60 << 20),
            name="cg_step",
        )(*inputs)
        return tuple(turn(result[i * params:(i + 1) * params]) for i in range(3))

    spec = P(("nodes", "cams"), None, None)
    split_last = P(None, ("nodes", "cams"))
    return jax.shard_map(
        on_device,
        mesh=mesh,
        in_specs=(spec, spec, spec, spec, P("nodes", None, None), split_last, split_last, split_last, spec),
        out_specs=(spec, spec, spec),
        check_vma=False,
    )
```
